128 devices in a mesh: seq: 32 (over x, z, core), head: 4 (over y).
Axes of the slice: x: 4, y: 4, z: 4, core: 2. Of those that a mesh axis runs over, the one named last changes fastest.
Arguments:
- patches: bfloat16 [131072, 768], P('seq'), may hold values from -6 to 6
- slot_image: int32 [512], P('seq'), may hold values from -1 to 255, as said below
- slot_dest: int32 [512], P('seq'), may hold values from -1 to 255, as said below
- enc_gain: float32 [768], replicated, may hold values from 0.1 to 1.9
- w_qkv: bfloat16 [3, 768, 768], P(None, None, 'head'), may hold values from -1.2 to 1.2
- w_out: bfloat16 [768, 768], P('head'), may hold values from -0.21875 to 0.21875
- fast_gain: float32 [768], replicated, may hold values from 0.1 to 1.9
- w_fast: bfloat16 [3, 768, 768], P(None, None, 'head'), may hold values from -0.21875 to 0.21875
- w_rate: bfloat16 [768, 4], P(None, 'head'), may hold values from -0.21875 to 0.21875
- fast_gate_up: float32 [4, 2, 192, 384], P('head'), may hold values from -0.4375 to 0.4375
- fast_down: float32 [4, 384, 192], P('head'), may hold values from -0.3125 to 0.3125
Outputs:
- view_out: bfloat16 [65536, 768], P('seq', 'head')
The draws below stay inside these ranges and needn't reach their ends.
Inputs may be any that keep to these rules, and one draw needn't show every extreme that they name: slot_dest gives for each slot the view-order block that its block becomes, or -1 for an empty slot; every view-order block is named by exactly one slot. Slots 2i and 2i + 1 of one seq index are both empty or name view blocks 2m and 2m + 1. The slots of one seq index name at most 2 blocks of any one view shard (blocks s * 8 to (s + 1) * 8 - 1), and some seq index uses all of its slots. slot_image is -1 exactly where slot_dest is -1; an image is one block or the two blocks of a slot pair, and different images have different ids.
All inputs are finite; a program needn't handle non-finite values.
Results may differ from the reference program's by a relative error of at most 0.035.
Values may be sent and summed in bfloat16 or wider, within the bound.
No kernel may reach another device: no remote copies, remote signals or barrier semaphores. Data moves between devices by JAX's collectives and lax.ppermute only.
A program may use at most 128 MiB of HBM per device.

```python
import math
import jax
import jax.numpy as jnp
from jax import lax

D = 768
HDIM = 64
FHEADS = 4
FW = 192
FH = 384
BLK = 256
BLK_DEV = 8
WSLOT = 16
VTOKENS = 65536
WTOKENS = 131072
N_SEQ = 32


def source_rank(source, busiest):
    half_away = (busiest + N_SEQ // 2) % N_SEQ
    next_one = (busiest + 1) % N_SEQ
    rotated = (source - busiest - 2) % N_SEQ
    rest = jnp.where(rotated < N_SEQ // 2 - 2, rotated + 2, rotated + 1)
    return jnp.where(source == half_away, 0, jnp.where(source == next_one, 1, rest))


def slot_layout(key):
    key_parts = jax.random.split(jax.random.fold_in(key, 41), 5)
    bins_dev = BLK_DEV // 2
    busiest = jax.random.randint(key_parts[0], (), 0, N_SEQ)
    shifts = jax.random.permutation(key_parts[2], N_SEQ - 1)
    paired = jax.random.randint(key_parts[3], (N_SEQ, bins_dev), 0, 2)
    places = jax.vmap(lambda part_key: jax.random.permutation(part_key, BLK_DEV))(jax.random.split(key_parts[4], N_SEQ))
    source = jnp.broadcast_to(jnp.arange(N_SEQ, dtype=jnp.int32)[:, None], (N_SEQ, bins_dev))
    column = jnp.broadcast_to(jnp.arange(bins_dev, dtype=jnp.int32)[None, :], (N_SEQ, bins_dev))
    ordinal = column * N_SEQ + source_rank(source, busiest)
    to_busiest = ordinal < BLK_DEV
    offset_bin = shifts[column % (N_SEQ - 1)]
    spread_to = (busiest + 1 + (source + offset_bin) % (N_SEQ - 1)) % N_SEQ
    worker = jnp.where(to_busiest, busiest, spread_to)
    place_bin = jnp.where(to_busiest, ordinal, 2 * column + (source == N_SEQ - 1).astype(jnp.int32))
    place_bin = places[worker, place_bin]
    view_first = source * BLK_DEV + 2 * column
    slot_first = worker * (2 * BLK_DEV) + 2 * place_bin
    second_image = jnp.where(paired == 1, view_first, view_first + 1)
    slot_all = jnp.concatenate([slot_first.reshape(-1), slot_first.reshape(-1) + 1]).astype(jnp.int32)
    view_all = jnp.concatenate([view_first.reshape(-1), view_first.reshape(-1) + 1]).astype(jnp.int32)
    image_all = jnp.concatenate([view_first.reshape(-1), second_image.reshape(-1)]).astype(jnp.int32)
    unused = jnp.full((N_SEQ * 2 * BLK_DEV,), -1, jnp.int32)
    return (unused.at[slot_all].set(image_all), unused.at[slot_all].set(view_all))


def draw_slot_image(key, part):
    return slot_layout(key)[0]


def draw_slot_dest(key, part):
    return slot_layout(key)[1]


def draw_w_qkv(key, part):
    key_parts = jax.random.split(jax.random.fold_in(key, 77), 1)
    spread = D ** (-0.5)
    weights = jax.random.normal(key_parts[0], (3, D, D), jnp.float32) * spread
    return jnp.clip(weights, -1.15, 1.15).astype(jnp.bfloat16)


def block_scale(own_key, shape, cuts, smallest, largest):
    factor_of = 1.0
    for position, shards_of in cuts:
        steps = jax.random.uniform(jax.random.fold_in(jax.random.fold_in(own_key, 6), position), (shards_of,), jnp.float32, smallest / len(cuts), largest / len(cuts))
        factor_of = factor_of * jnp.repeat(jnp.exp(steps), shape[position] // shards_of).reshape((-1,) + (1,) * (len(shape) - 1 - position))
    return factor_of


def scatter_about(rng, shape, scale, reach, shards=(), kind=jnp.bfloat16):
    array = scale * jax.random.normal(rng, shape, jnp.float32)
    if shards:
        array = array * block_scale(rng, shape, shards, -0.22, 0.18)
    return jnp.clip(array, -reach, reach).astype(kind)


def setup_inputs(seed: int = 0) -> dict:
    seeds = jax.random.split(jax.random.key(seed), 12)
    return {
        "patches": scatter_about(seeds[0], (WTOKENS, D), 1.0, 6.0, ((0, 32),)),
        "slot_image": draw_slot_image(jax.random.fold_in(seeds[11], 71), 0),
        "slot_dest": draw_slot_dest(jax.random.fold_in(seeds[11], 71), 0),
        "enc_gain": jnp.clip(1.0 + 0.18 * jax.random.normal(seeds[3], (D,), jnp.float32), 0.1, 1.9),
        "w_qkv": draw_w_qkv(jax.random.fold_in(seeds[11], 71), 0),
        "w_out": scatter_about(seeds[5], (D, D), D ** -0.5, 0.21875, ((0, 4),)),
        "fast_gain": jnp.clip(1.0 + 0.18 * jax.random.normal(seeds[6], (D,), jnp.float32), 0.1, 1.9),
        "w_fast": scatter_about(seeds[7], (3, D, D), D ** -0.5, 0.21875, ((2, 4),)),
        "w_rate": scatter_about(seeds[8], (D, FHEADS), D ** -0.5, 0.21875, ((1, 4),)),
        "fast_gate_up": scatter_about(seeds[9], (FHEADS, 2, FW, FH), FW ** -0.5, 0.4375, ((0, 4),), jnp.float32),
        "fast_down": scatter_about(seeds[10], (FHEADS, FH, FW), FH ** -0.5, 0.3125, ((0, 4),), jnp.float32),
    }


EPSILON = 1e-06
RATE_SCALE = 0.1

def norm_rows(values, gain_vector):
    widened = values.astype(jnp.float32)
    factor = lax.rsqrt(lax.optimization_barrier(jnp.mean(widened * widened, axis=-1, keepdims=True)) + EPSILON)
    return (widened * factor * gain_vector.astype(jnp.float32)).astype(jnp.bfloat16)

def attend_pair(pieces):
    query_rows, key_rows, value_rows, token_ids = pieces
    token_count = query_rows.shape[0]
    heads_here = query_rows.shape[1] // HDIM
    q_heads = query_rows.astype(jnp.float32).reshape(token_count, heads_here, HDIM)
    k_heads = key_rows.astype(jnp.float32).reshape(token_count, heads_here, HDIM)
    v_heads = value_rows.astype(jnp.float32).reshape(token_count, heads_here, HDIM)
    scores = jnp.einsum('qhe,khe->hqk', q_heads, k_heads) * HDIM ** (-0.5)
    allowed = token_ids[:, None] == token_ids[None, :]
    scores = jnp.where(allowed[None], scores, -1e+30)
    top_score = lax.optimization_barrier(jnp.max(scores, axis=-1, keepdims=True))
    exp_scores = jnp.exp(scores - top_score)
    weights = (exp_scores / lax.optimization_barrier(jnp.sum(exp_scores, axis=-1, keepdims=True))).astype(jnp.bfloat16)
    mixed_heads = jnp.einsum('hqk,khe->qhe', weights.astype(jnp.float32), v_heads)
    return mixed_heads.astype(jnp.bfloat16).reshape(token_count, heads_here * HDIM)

def encode_group(rows_here, ids_here, enc_gain, w_qkv, w_out):
    normed = norm_rows(rows_here, enc_gain)
    projected = [jnp.dot(normed, w_qkv[which_one], preferred_element_type=jnp.float32).astype(jnp.bfloat16) for which_one in range(3)]
    span = 2 * BLK
    pair_count = rows_here.shape[0] // span
    attended = lax.map(attend_pair, (projected[0].reshape(pair_count, span, D), projected[1].reshape(pair_count, span, D), projected[2].reshape(pair_count, span, D), ids_here.reshape(pair_count, span)))
    attended = attended.reshape(rows_here.shape[0], D)
    head_total = jnp.zeros((rows_here.shape[0], D), jnp.float32)
    for group_index in range(FHEADS):
        block_cols = attended[:, group_index * FW:(group_index + 1) * FW]
        product = jnp.dot(block_cols, w_out[group_index * FW:(group_index + 1) * FW], preferred_element_type=jnp.float32)
        rounded = lax.optimization_barrier(product.astype(jnp.bfloat16))
        head_total = head_total + rounded.astype(jnp.float32)
    return (rows_here.astype(jnp.float32) + head_total).astype(jnp.bfloat16)

def renorm(updated, initial):
    target_norm = jnp.sqrt(lax.optimization_barrier(jnp.sum(initial * initial, axis=1, keepdims=True)))
    return updated * target_norm * lax.rsqrt(lax.optimization_barrier(jnp.sum(updated * updated, axis=1, keepdims=True)) + EPSILON)

def reference(patches, slot_image, slot_dest, enc_gain, w_qkv, w_out, fast_gain, w_fast, w_rate, fast_gate_up, fast_down):
    view_count = N_SEQ * BLK_DEV
    slot_total = N_SEQ * WSLOT
    target = jnp.where(slot_dest >= 0, slot_dest, view_count).astype(jnp.int32)
    view_blocks = jnp.zeros((view_count + 1, BLK, D), patches.dtype).at[target].set(patches.reshape(slot_total, BLK, D))[:view_count]
    view_ids = jnp.zeros((view_count + 1,), jnp.int32).at[target].set(slot_image.astype(jnp.int32))[:view_count]
    pair_total = view_count // 2
    group_size = math.gcd(8, pair_total)
    group_rows = view_blocks.reshape(pair_total // group_size, group_size * 2 * BLK, D)
    group_ids = jnp.repeat(view_ids, BLK).reshape(pair_total // group_size, group_size * 2 * BLK)
    embedded = lax.map(lambda pieces: encode_group(pieces[0], pieces[1], enc_gain, w_qkv, w_out), (group_rows, group_ids))
    embedded = embedded.reshape(view_count * BLK, D)
    normed_fast = norm_rows(embedded, fast_gain)
    fast_query = jnp.dot(normed_fast, w_fast[0], preferred_element_type=jnp.float32).astype(jnp.bfloat16)
    fast_key = jnp.dot(normed_fast, w_fast[1], preferred_element_type=jnp.float32).astype(jnp.bfloat16)
    fast_value = jnp.dot(normed_fast, w_fast[2], preferred_element_type=jnp.float32).astype(jnp.bfloat16)
    rate_all = RATE_SCALE * jax.nn.softplus(jnp.dot(normed_fast, w_rate, preferred_element_type=jnp.float32)) * VTOKENS ** (-0.5)
    columns_out = []
    for fast_head in range(FHEADS):
        chosen = slice(fast_head * FW, (fast_head + 1) * FW)
        key_here = fast_key[:, chosen]
        query_here = fast_query[:, chosen]
        gate_init = fast_gate_up[fast_head, 0]
        up_init = fast_gate_up[fast_head, 1]
        down_init = fast_down[fast_head]
        gate_half = gate_init.astype(jnp.bfloat16)
        up_half = up_init.astype(jnp.bfloat16)
        down_half = down_init.astype(jnp.bfloat16)
        key_gate = jnp.dot(key_here, gate_half, preferred_element_type=jnp.float32)
        key_up = jnp.dot(key_here, up_half, preferred_element_type=jnp.float32)
        hidden_key = (jax.nn.silu(key_gate) * key_up).astype(jnp.bfloat16)
        out_grad = (-rate_all[:, fast_head:fast_head + 1] * fast_value[:, chosen].astype(jnp.float32)).astype(jnp.bfloat16)
        grad_down = jnp.dot(hidden_key.T, out_grad, preferred_element_type=jnp.float32)
        hidden_grad = jnp.dot(out_grad, down_half.T, preferred_element_type=jnp.float32)
        sigmoid_gate = jax.nn.sigmoid(key_gate)
        gate_grad = (hidden_grad * key_up * sigmoid_gate * (1.0 + key_gate * (1.0 - sigmoid_gate))).astype(jnp.bfloat16)
        up_grad = (hidden_grad * jax.nn.silu(key_gate)).astype(jnp.bfloat16)
        grad_gate = jnp.dot(key_here.T, gate_grad, preferred_element_type=jnp.float32)
        grad_up = jnp.dot(key_here.T, up_grad, preferred_element_type=jnp.float32)
        applied_gate = renorm(gate_init - grad_gate, gate_init).astype(jnp.bfloat16)
        applied_up = renorm(up_init - grad_up, up_init).astype(jnp.bfloat16)
        applied_down = renorm(down_init - grad_down, down_init).astype(jnp.bfloat16)
        query_gate = jnp.dot(query_here, applied_gate, preferred_element_type=jnp.float32)
        query_up = jnp.dot(query_here, applied_up, preferred_element_type=jnp.float32)
        query_hidden = (jax.nn.silu(query_gate) * query_up).astype(jnp.bfloat16)
        fast_out = jnp.dot(query_hidden, applied_down, preferred_element_type=jnp.float32)
        columns_out.append((embedded[:, chosen].astype(jnp.float32) + fast_out).astype(jnp.bfloat16))
    return jnp.concatenate(columns_out, axis=1)
```

```python
import jax
import jax.numpy as jnp
from jax import lax
from jax.experimental import pallas as pl
from jax.experimental.pallas import tpu as pltpu
from jax.sharding import Mesh, PartitionSpec as P

D = 768
HDIM = 64
BLK = 256
SPAN = 512
FW = 192
FH = 384
SEQ = 32
HEADS = 4
PAIRS = 8
LT = 3
GT = 224
EPSILON = 1e-06
RATE_SCALE = 0.1
VTOKENS = 65536
BF = jnp.bfloat16
F32 = jnp.float32
SEQ_AXES = ("x", "z", "core")
ALL_AXES = ("x", "z", "core", "head")
PARAMS = pltpu.CompilerParams(vmem_limit_bytes=48 << 20)

ANY = pl.BlockSpec(memory_space=pl.ANY)
SMEM = pl.BlockSpec(memory_space=pltpu.SMEM)
VMEM = pl.BlockSpec(memory_space=pltpu.VMEM)


def mm(a, b):
    return jnp.dot(a, b, preferred_element_type=F32)


def mm_nt(a, b):
    return lax.dot_general(a, b, (((1,), (1,)), ((), ())), preferred_element_type=F32)


def mm_tn(a, b):
    return lax.dot_general(a, b, (((0,), (0,)), ((), ())), preferred_element_type=F32)


def norm(rows, gain):
    factor = lax.rsqrt(jnp.mean(rows * rows, axis=-1, keepdims=True) + EPSILON)
    return (rows * factor * gain).astype(BF)


def spread_body(where_ref, x_ref, meta_ref, o_ref, sem):
    parity = where_ref[0]
    half = where_ref[1]
    for p in range(PAIRS):
        for t in range(LT):
            pltpu.make_async_copy(
                x_ref.at[
                    pl.ds(p * 64 + parity * 32, SEQ),
                    :,
                    pl.ds(pl.multiple_of(half * FH + t * 128, 128), 128),
                ],
                o_ref.at[:, p * LT + t],
                sem,
            ).start()
    pltpu.make_async_copy(meta_ref, o_ref.at[:, PAIRS * LT], sem).start()
    pltpu.make_async_copy(o_ref, o_ref, sem).wait()


def spread(where, x, meta):
    return pl.pallas_call(
        spread_body,
        out_shape=jax.ShapeDtypeStruct((SEQ, PAIRS * LT + 1, 8, 128), BF),
        in_specs=[SMEM, ANY, ANY],
        out_specs=ANY,
        scratch_shapes=[pltpu.SemaphoreType.DMA(())],
        compiler_params=PARAMS,
        name="spread",
    )(where, x, meta)


def pick_body(dest_ref, x_ref, o_ref, sem):
    def step(q, carry):
        first = dest_ref[q]

        @pl.when(first >= 0)
        def _():
            pltpu.make_async_copy(
                x_ref.at[q // PAIRS, pl.ds((q % PAIRS) * LT, LT)],
                o_ref.at[jnp.minimum(first // 2, SEQ * HEADS - 1)],
                sem,
            ).start()

        return carry

    lax.fori_loop(0, SEQ * PAIRS, step, 0, unroll=8)
    pltpu.make_async_copy(o_ref, o_ref, sem).wait()


def pick(dest, x):
    return pl.pallas_call(
        pick_body,
        out_shape=jax.ShapeDtypeStruct((SEQ * HEADS, LT, 8, 128), BF),
        in_specs=[SMEM, ANY],
        out_specs=ANY,
        scratch_shapes=[pltpu.SemaphoreType.DMA(())],
        compiler_params=PARAMS,
        name="pick",
    )(dest, x)


def encode_body(flag_ref, x_ref, gain_ref, wqkv_ref, wout_ref, o_ref, xs, ns, att):
    flip = flag_ref[0]
    bias = jnp.where(flag_ref[1] != 0, 0.0, -1e30).astype(F32)
    for b in range(2):
        base = pl.multiple_of(jnp.bitwise_xor(flip, b) * BLK, BLK)
        for c in range(2):
            for t in range(LT):
                xs[pl.ds(base, BLK), pl.ds(c * FH + t * 128, 128)] = (
                    x_ref[:, 2 * b + c, t].astype(F32).reshape(BLK, 128)
                )
    gain = gain_ref[...]
    for r in range(4):
        ns[pl.ds(r * 128, 128), :] = norm(xs[pl.ds(r * 128, 128), :], gain)
    for g in range(HEADS):
        y = mm(ns[:, :FH], wqkv_ref[0, g]) + mm(ns[:, FH:], wqkv_ref[1, g])
        q_all = (y[:, :FW] * HDIM**-0.5).astype(BF)
        k_all = y[:, FW : 2 * FW].astype(BF)
        v_all = y[:, 2 * FW :].astype(BF)
        for j in range(FW // HDIM):
            cut = slice(j * HDIM, (j + 1) * HDIM)
            k, v = k_all[:, cut], v_all[:, cut]
            for b in range(2):
                rows = slice(b * BLK, (b + 1) * BLK)
                other = slice((1 - b) * BLK, (2 - b) * BLK)
                q = q_all[rows, cut]
                s_own = mm_nt(q, k[rows])
                s_off = mm_nt(q, k[other]) + bias
                top = jnp.maximum(
                    jnp.max(s_own, axis=-1, keepdims=True), jnp.max(s_off, axis=-1, keepdims=True)
                )
                p_own = jnp.exp(s_own - top)
                p_off = jnp.exp(s_off - top)
                total = jnp.sum(p_own, axis=-1, keepdims=True) + jnp.sum(
                    p_off, axis=-1, keepdims=True
                )
                o = mm(p_own.astype(BF), v[rows]) + mm(p_off.astype(BF), v[other])
                att[rows, pl.ds((g * 3 + j) * HDIM, HDIM)] = (o / total).astype(BF)
    for c in range(2):
        mixed = mm(att[...], wout_ref[c].reshape(D, FH))
        o_ref[:, pl.ds(c * FH, FH)] = (xs[:, pl.ds(c * FH, FH)] + mixed).astype(BF)


def encode(flags, x, gain, wqkv, wout):
    return pl.pallas_call(
        encode_body,
        out_shape=jax.ShapeDtypeStruct((SPAN, D), BF),
        in_specs=[SMEM, VMEM, VMEM, VMEM, VMEM],
        out_specs=VMEM,
        scratch_shapes=[
            pltpu.VMEM((SPAN, D), F32),
            pltpu.VMEM((SPAN, D), BF),
            pltpu.VMEM((SPAN, D), BF),
        ],
        compiler_params=PARAMS,
        name="encode",
    )(flags, x, gain, wqkv, wout)


def make_fast_body(chunks, first, last):
    def body(*refs):
        rows_in = refs[:chunks]
        gain_ref, pick_ref, w_ref, rate_ref, init_ref = refs[chunks : chunks + 5]
        at = chunks + 5
        if not first:
            sum_ref = refs[at]
            at += 1
        q_refs = refs[at : at + chunks]
        e_refs = refs[at + chunks : at + 2 * chunks]
        g_ref = refs[at + 2 * chunks]
        gain = gain_ref[...]
        total_gu = total_d = None
        for x_ref, q_ref, e_ref in zip(rows_in, q_refs, e_refs):
            x = x_ref[...]
            n = norm(x.astype(F32), gain)
            e_ref[...] = mm(x, pick_ref[...]).astype(BF)
            q_ref[...] = mm(n, w_ref[0]).astype(BF)
            key = mm(n, w_ref[1]).astype(BF)
            value = mm(n, w_ref[2]).astype(BF).astype(F32)
            z = mm(n, rate_ref[...])
            soft = jnp.maximum(z, 0.0) + jnp.log1p(jnp.exp(-jnp.abs(z)))
            out_grad = (-(RATE_SCALE * VTOKENS**-0.5) * soft * value).astype(BF)
            gate = mm(key, init_ref[:, :FH])
            up = mm(key, init_ref[:, FH : 2 * FH])
            hidden_grad = mm(out_grad, init_ref[:, 2 * FH :])
            s = jax.nn.sigmoid(gate)
            silu = gate * s
            hidden = (silu * up).astype(BF)
            gate_grad = (hidden_grad * up * s * (1.0 + gate * (1.0 - s))).astype(BF)
            up_grad = (hidden_grad * silu).astype(BF)
            gu = mm_tn(key, jnp.concatenate([gate_grad, up_grad], axis=1))
            dn = mm_tn(out_grad, hidden)
            total_gu = gu if total_gu is None else total_gu + gu
            total_d = dn if total_d is None else total_d + dn
        if not first:
            total_gu = total_gu + sum_ref[:, : 2 * FH]
            total_d = total_d + sum_ref[:, 2 * FH :]
        if last:
            for t in range(6):
                g_ref[pl.ds(t * 24, 24)] = (
                    total_gu[:, t * 128 : (t + 1) * 128].astype(BF).reshape(24, 8, 128)
                )
            for t in range(3):
                g_ref[pl.ds((6 + t) * 24, 24)] = (
                    total_d[:, t * 128 : (t + 1) * 128].astype(BF).reshape(24, 8, 128)
                )
            g_ref[pl.ds(216, 8)] = jnp.zeros((8, 8, 128), BF)
        else:
            g_ref[:, : 2 * FH] = total_gu
            g_ref[:, 2 * FH :] = total_d

    return body


def fast(rows_in, shared, sums, last):
    chunks = len(rows_in)
    first = sums is None
    operands = (*rows_in, *shared) + (() if first else (sums,))
    sizes = [jax.ShapeDtypeStruct((r.shape[0], FW), BF) for r in rows_in]
    grad = (
        jax.ShapeDtypeStruct((GT, 8, 128), BF)
        if last
        else jax.ShapeDtypeStruct((FW, 3 * FH), F32)
    )
    outs = pl.pallas_call(
        make_fast_body(chunks, first, last),
        out_shape=(*sizes, *sizes, grad),
        in_specs=[VMEM] * len(operands),
        out_specs=[VMEM] * (2 * chunks + 1),
        compiler_params=PARAMS,
        name="fast_grad",
    )(*operands)
    return outs[:chunks], outs[chunks : 2 * chunks], outs[-1]


def sum_body(x_ref, o_ref):
    total = x_ref[0].astype(F32)
    for i in range(1, SEQ):
        total = total + x_ref[i].astype(F32)
    total = total.astype(BF)
    for i in range(SEQ):
        o_ref[i] = total


def sum_pieces(x):
    return pl.pallas_call(
        sum_body,
        out_shape=jax.ShapeDtypeStruct(x.shape, BF),
        in_specs=[VMEM],
        out_specs=VMEM,
        compiler_params=PARAMS,
        name="sum_pieces",
    )(x)


def renorm(updated, initial, axis):
    target = jnp.sqrt(jnp.sum(initial * initial, axis=axis, keepdims=True))
    return updated * target * lax.rsqrt(jnp.sum(updated * updated, axis=axis, keepdims=True) + EPSILON)


def make_apply_body(starts):
    def body(head_ref, g_ref, init_ref, *refs):
        n = len(starts)
        q_refs, e_refs = refs[:n], refs[n : 2 * n]
        o_ref, gs, ws = refs[2 * n :]
        for t in range(9):
            gs[:, pl.ds(t * 128, 128)] = g_ref[pl.ds(t * 24, 24)].astype(F32).reshape(FW, 128)
        for part, axis in ((0, 1), (1, 1), (2, 0)):
            cut = pl.ds(part * FH, FH)
            init = init_ref[:, cut]
            ws[:, cut] = renorm(init - gs[:, cut], init, axis).astype(BF)
        for (shift, offset), q_ref, e_ref in zip(starts, q_refs, e_refs):
            q = q_ref[...]
            gate = mm(q, ws[:, :FH])
            up = mm(q, ws[:, FH : 2 * FH])
            hidden = (gate * jax.nn.sigmoid(gate) * up).astype(BF)
            out = e_ref[...].astype(F32) + mm_nt(hidden, ws[:, 2 * FH :])
            base = pl.multiple_of(lax.rem(head_ref[0] + shift, HEADS) * SPAN + offset, BLK)
            o_ref[pl.ds(base, q.shape[0]), :] = out.astype(BF)

    return body


def apply(head, grads, init, queries, columns, starts):
    return pl.pallas_call(
        make_apply_body(starts),
        out_shape=jax.ShapeDtypeStruct((HEADS * SPAN, FW), BF),
        in_specs=[SMEM] + [VMEM] * (2 + 2 * len(queries)),
        out_specs=VMEM,
        scratch_shapes=[pltpu.VMEM((FW, 3 * FH), F32), pltpu.VMEM((FW, 3 * FH), BF)],
        compiler_params=PARAMS,
        name="apply_fast",
    )(head, grads, init, *queries, *columns)


def exchange(x, axes):
    return lax.all_to_all(x, axes, split_axis=0, concat_axis=0, tiled=True)


def shifted(x, by):
    return lax.ppermute(x, "head", [(i, (i + by) % HEADS) for i in range(HEADS)])


def on_device(
    patches,
    slot_image,
    slot_dest,
    enc_gain,
    w_qkv,
    w_out,
    fast_gain,
    w_fast,
    w_rate,
    fast_gate_up,
    fast_down,
):
    head = lax.axis_index("head")
    core = lax.axis_index("core")
    seq = lax.axis_index(SEQ_AXES)

    wide = jnp.concatenate([w_qkv[0], w_qkv[1], w_qkv[2]], axis=1)
    qkv_half = lax.dynamic_slice_in_dim(wide, core * FH, FH, 0)
    out_half = jnp.where(core == 0, w_out[:, :FH], w_out[:, FH:])
    wqkv = lax.all_gather(qkv_half, ("core", "head"), axis=0, tiled=False)
    wout = lax.all_gather(out_half, ("core", "head"), axis=0, tiled=False)
    wqkv = wqkv.reshape(2, HEADS, FH, 3 * FW)
    wout = wout.reshape(2, HEADS, FW, FH)

    where = jnp.stack([head // 2, head % 2]).astype(jnp.int32)
    ids = jnp.stack([slot_dest, slot_image]).astype(BF)
    tile = jnp.zeros((8, 128), BF).at[:2, :16].set(ids)
    meta = jnp.broadcast_to(tile[None], (SEQ, 8, 128))
    pieces = exchange(spread(where, patches.reshape(-1, 8, D), meta), SEQ_AXES)

    ids_all = pieces[:, PAIRS * LT, :2, :16].astype(jnp.int32)
    first = ids_all[:, 0, 0::2].reshape(-1)
    mine = exchange(pick(first, pieces), ALL_AXES)

    same = (ids_all[:, 1, 0::2] == ids_all[:, 1, 1::2]).reshape(-1)
    here = (first // 2 == seq * HEADS + head) & (first >= 0)
    flags = jnp.stack(
        [jnp.sum(jnp.where(here, first % 2, 0)), jnp.sum(jnp.where(here & same, 1, 0))]
    ).astype(jnp.int32)

    embedded = encode(
        flags, mine.reshape(SEQ, 4, LT, 8, 128), enc_gain.reshape(1, D), wqkv, wout
    )

    before = shifted(embedded, 1)
    after = shifted(embedded, -1)
    init = jnp.concatenate([fast_gate_up[0, 0], fast_gate_up[0, 1], fast_down[0].T], axis=1)
    pick_cols = (jnp.arange(D)[:, None] == head * FW + jnp.arange(FW)[None, :]).astype(BF)
    shared = (
        fast_gain.reshape(1, D),
        pick_cols,
        w_fast,
        jnp.broadcast_to(w_rate, (D, FW)),
        init.astype(BF),
    )
    q0, e0, sums = fast((embedded,), shared, None, False)
    far_low = shifted(after[:BLK], -1)
    far_high = shifted(before[BLK:], 1)
    q1, e1, sums = fast((before, after), shared, sums, False)
    q2, e2, grads = fast((far_low, far_high), shared, sums, True)

    summed = sum_pieces(exchange(grads, SEQ_AXES).reshape(SEQ, GT // SEQ, 8, 128))
    whole = exchange(summed, SEQ_AXES).reshape(GT, 8, 128)
    starts = ((0, 0), (3, 0), (1, 0), (2, 0), (2, BLK))
    return apply(
        head.astype(jnp.int32).reshape(1),
        whole,
        init,
        (*q0, *q1, *q2),
        (*e0, *e1, *e2),
        starts,
    )


def solution(mesh):
    fine = Mesh(mesh.devices.reshape(4, 4, 2, HEADS), ALL_AXES)
    in_specs = (
        P(SEQ_AXES, None),
        P(SEQ_AXES),
        P(SEQ_AXES),
        P(),
        P(None, None, "head"),
        P("head", None),
        P(),
        P(None, None, "head"),
        P(None, "head"),
        P("head", None, None, None),
        P("head", None, None),
    )
    return jax.shard_map(
        on_device, mesh=fine, in_specs=in_specs, out_specs=P(SEQ_AXES, "head"), check_vma=False
    )
```

```python
import jax
import jax.numpy as jnp
from jax import lax
from jax.experimental import pallas as pl
from jax.experimental.pallas import tpu as pltpu
from jax.sharding import Mesh, PartitionSpec as P

D = 768
HDIM = 64
BLK = 256
SPAN = 512
FW = 192
FH = 384
SEQ = 32
HEADS = 4
PAIRS = 8
LT = 3
GT = 224
EPSILON = 1e-06
LOG2E = 1.4426950408889634
RATE_SCALE = 0.1
VTOKENS = 65536
BF = jnp.bfloat16
F32 = jnp.float32
SEQ_AXES = ("x", "z", "core")
ALL_AXES = ("x", "z", "core", "head")
PARAMS = pltpu.CompilerParams(vmem_limit_bytes=48 << 20)

ANY = pl.BlockSpec(memory_space=pl.ANY)
SMEM = pl.BlockSpec(memory_space=pltpu.SMEM)
VMEM = pl.BlockSpec(memory_space=pltpu.VMEM)


def mm(a, b):
    return jnp.dot(a, b, preferred_element_type=F32)


def mm_nt(a, b):
    return lax.dot_general(a, b, (((1,), (1,)), ((), ())), preferred_element_type=F32)


def mm_tn(a, b):
    return lax.dot_general(a, b, (((0,), (0,)), ((), ())), preferred_element_type=F32)


def norm(rows, gain):
    factor = lax.rsqrt(jnp.mean(rows * rows, axis=-1, keepdims=True) + EPSILON)
    return (rows * factor * gain).astype(BF)


def spread_body(where_ref, x_ref, meta_ref, o_ref, buf, sems):
    parity = where_ref[0]
    half = where_ref[1]
    copies = []
    for p in range(PAIRS):
        copies.append(
            pltpu.make_async_copy(
                x_ref.at[
                    pl.ds(p * 64 + parity * 32, SEQ), :, pl.ds(pl.multiple_of(half * FH, 128), FH)
                ],
                buf.at[p],
                sems.at[p],
            )
        )
        copies[p].start()
    o_ref[:, PAIRS * LT] = jnp.broadcast_to(meta_ref[...][None], (SEQ, 8, 128))
    for p in range(PAIRS):
        copies[p].wait()
        for t in range(LT):
            o_ref[:, p * LT + t] = buf[p, :, :, t * 128 : (t + 1) * 128]


def spread(where, x, meta):
    return pl.pallas_call(
        spread_body,
        out_shape=jax.ShapeDtypeStruct((SEQ, PAIRS * LT + 1, 8, 128), BF),
        in_specs=[SMEM, ANY, VMEM],
        out_specs=VMEM,
        scratch_shapes=[
            pltpu.VMEM((PAIRS, SEQ, 8, FH), BF),
            pltpu.SemaphoreType.DMA((PAIRS,)),
        ],
        compiler_params=PARAMS,
        name="spread",
    )(where, x, meta)


def pick_body(dest_ref, x_ref, o_ref, sem):
    def step(q, carry):
        first = dest_ref[q]

        @pl.when(first >= 0)
        def _():
            pltpu.make_async_copy(
                x_ref.at[q // PAIRS, pl.ds((q % PAIRS) * LT, LT)],
                o_ref.at[jnp.minimum(first // 2, SEQ * HEADS - 1)],
                sem,
            ).start()

        return carry

    lax.fori_loop(0, SEQ * PAIRS, step, 0, unroll=8)
    pltpu.make_async_copy(o_ref, o_ref, sem).wait()


def pick(dest, x):
    return pl.pallas_call(
        pick_body,
        out_shape=jax.ShapeDtypeStruct((SEQ * HEADS, LT, 8, 128), BF),
        in_specs=[SMEM, ANY],
        out_specs=ANY,
        scratch_shapes=[pltpu.SemaphoreType.DMA(())],
        compiler_params=PARAMS,
        name="pick",
    )(dest, x)


def attend(block, bias, q_ref, k_ref, v_ref, att):
    own = slice(block * BLK, (block + 1) * BLK)
    row = lax.broadcasted_iota(jnp.int32, (FW, BLK), 0)
    ones = jnp.ones((16, SPAN), BF)
    for g in range(HEADS):
        k = k_ref[g]
        q = q_ref[g]
        for j in range(FW // HDIM):
            mine = (row >= j * HDIM) & (row < (j + 1) * HDIM)
            s = mm(k, jnp.where(mine, q, jnp.zeros_like(q)))
            parts = [s[:BLK], s[BLK:]]
            parts[1 - block] = parts[1 - block] + bias
            top = jnp.max(jnp.maximum(parts[0], parts[1]), axis=0, keepdims=True)
            p = jnp.concatenate([jnp.exp2(x - top).astype(BF) for x in parts], axis=0)
            v = jnp.concatenate([v_ref[g, j * HDIM : (j + 1) * HDIM], ones], axis=0)
            o = mm(v, p)
            o = (o[:HDIM] * (1.0 / o[HDIM : HDIM + 1])).astype(BF)
            for at in range(0, HDIM, 32):
                half, rest = divmod(j * HDIM + at, 96)
                att[pl.ds(half * FH + g * 96 + rest, 32), :] = o[at : at + 32]


def encode_first_body(
    flag_ref, x_ref, gain_ref, w_ref, o_ref, q_ref, k_ref, v_ref, rest_ref, xs, ns, att, q0, ws, sems
):
    copies = [
        pltpu.make_async_copy(w_ref.at[:, g], ws.at[g], sems.at[g]) for g in range(HEADS)
    ]
    for c in copies:
        c.start()
    flip = flag_ref[0]
    bias = jnp.where(flag_ref[1] != 0, 0.0, -1e30).astype(F32)
    for b in range(2):
        base = pl.multiple_of(jnp.bitwise_xor(flip, b) * BLK, BLK)
        for c in range(2):
            for t in range(LT):
                xs[pl.ds(base, BLK), pl.ds(c * FH + t * 128, 128)] = (
                    x_ref[:, 2 * b + c, t].astype(F32).reshape(BLK, 128)
                )
    gain = gain_ref[...]
    for r in range(8):
        ns[pl.ds(r * 64, 64), :] = norm(xs[pl.ds(r * 64, 64), :], gain)
    rest_ref[...] = xs[BLK:, :].astype(BF)
    n = ns[...]
    scale = HDIM**-0.5 * LOG2E
    for g in range(HEADS):
        copies[g].wait()
        w = ws[g, :, : 3 * 96].reshape(3 * FW, D)
        q = (mm_nt(w[:FW], n) * scale).astype(BF)
        q0[g] = q[:, :BLK]
        q_ref[g] = q[:, BLK:]
        k_ref[g] = mm_nt(n, w[FW : 2 * FW]).astype(BF)
        v_ref[g] = mm_nt(w[2 * FW :], n).astype(BF)
    attend(0, bias, q0, k_ref, v_ref, att)
    out = xs[:BLK, :]
    for c in range(2):
        for g in range(HEADS):
            out = out + mm_tn(att[pl.ds(c * FH + g * 96, 96), :], ws[g, c, 3 * 96 :])
    o_ref[...] = out.astype(BF)


def encode_first(flags, x, gain, w):
    return pl.pallas_call(
        encode_first_body,
        out_shape=(
            jax.ShapeDtypeStruct((BLK, D), BF),
            jax.ShapeDtypeStruct((HEADS, FW, BLK), BF),
            jax.ShapeDtypeStruct((HEADS, SPAN, FW), BF),
            jax.ShapeDtypeStruct((HEADS, FW, SPAN), BF),
            jax.ShapeDtypeStruct((BLK, D), BF),
        ),
        in_specs=[SMEM, VMEM, VMEM, ANY],
        out_specs=[VMEM] * 5,
        scratch_shapes=[
            pltpu.VMEM((SPAN, D), F32),
            pltpu.VMEM((SPAN, D), BF),
            pltpu.VMEM((D, BLK), BF),
            pltpu.VMEM((HEADS, FW, BLK), BF),
            pltpu.VMEM((HEADS, 2, FH, D), BF),
            pltpu.SemaphoreType.DMA((HEADS,)),
        ],
        compiler_params=PARAMS,
        name="encode_first",
    )(flags, x, gain, w)


def encode_second_body(flag_ref, q_ref, k_ref, v_ref, rest_ref, w_ref, o_ref, att, ws, sem):
    copy = pltpu.make_async_copy(w_ref.at[:, :, pl.ds(3 * 96, 96)], ws, sem)
    copy.start()
    bias = jnp.where(flag_ref[1] != 0, 0.0, -1e30).astype(F32)
    attend(1, bias, q_ref, k_ref, v_ref, att)
    copy.wait()
    mixed = mm_tn(att[...], ws[...].reshape(D, D))
    o_ref[...] = (rest_ref[...].astype(F32) + mixed).astype(BF)


def encode_second(flags, q, k, v, rest, w):
    return pl.pallas_call(
        encode_second_body,
        out_shape=jax.ShapeDtypeStruct((BLK, D), BF),
        in_specs=[SMEM, VMEM, VMEM, VMEM, VMEM, ANY],
        out_specs=VMEM,
        scratch_shapes=[
            pltpu.VMEM((D, BLK), BF),
            pltpu.VMEM((2, HEADS, 96, D), BF),
            pltpu.SemaphoreType.DMA(()),
        ],
        compiler_params=PARAMS,
        name="encode_second",
    )(flags, q, k, v, rest, w)


def make_fast_body(chunks, first, last):
    def body(*refs):
        rows_in = refs[:chunks]
        gain_ref, w_ref, rate_ref, gu_ref, down_ref = refs[chunks : chunks + 5]
        sum_ref = None if first else refs[chunks + 5]
        g_ref = refs[-1]
        gain = gain_ref[...]
        gate_up = [gu_ref[i].astype(BF) for i in range(2)]
        down = down_ref[...].astype(BF)
        sums = None
        for x_ref in rows_in:
            n = norm(x_ref[...].astype(F32), gain)
            key = mm_nt(n, w_ref[1]).astype(BF)
            value = mm_nt(n, w_ref[2]).astype(BF).astype(F32)
            z = mm_nt(n, rate_ref[...])
            soft = jnp.maximum(z, 0.0) + jnp.log1p(jnp.exp(-jnp.abs(z)))
            out_grad = (-(RATE_SCALE * VTOKENS**-0.5) * soft * value).astype(BF)
            gate = mm(key, gate_up[0])
            up = mm(key, gate_up[1])
            hidden_grad = mm(out_grad, down)
            s = jax.nn.sigmoid(gate)
            silu = gate * s
            hidden = (silu * up).astype(BF)
            gate_grad = (hidden_grad * up * s * (1.0 + gate * (1.0 - s))).astype(BF)
            up_grad = (hidden_grad * silu).astype(BF)
            parts = [mm_tn(key, gate_grad), mm_tn(key, up_grad), mm_tn(out_grad, hidden)]
            sums = parts if sums is None else [a + b for a, b in zip(sums, parts)]
        for i, total in enumerate(sums):
            if not first:
                total = total + sum_ref[i]
            if last:
                for t in range(LT):
                    g_ref[pl.ds((i * LT + t) * 24, 24)] = (
                        total[:, t * 128 : (t + 1) * 128].astype(BF).reshape(24, 8, 128)
                    )
            else:
                g_ref[i] = total
        if last:
            g_ref[pl.ds(216, 8)] = jnp.zeros((8, 8, 128), BF)

    return body


def fast(rows_in, shared, sums, last):
    first = sums is None
    operands = (*rows_in, *shared) + (() if first else (sums,))
    return pl.pallas_call(
        make_fast_body(len(rows_in), first, last),
        out_shape=(
            jax.ShapeDtypeStruct((GT, 8, 128), BF)
            if last
            else jax.ShapeDtypeStruct((3, FW, FH), F32)
        ),
        in_specs=[VMEM] * len(operands),
        out_specs=VMEM,
        compiler_params=PARAMS,
        name="fast_grad",
    )(*operands)


def make_query_body(starts):
    def body(head_ref, gain_ref, w_ref, pick_ref, *refs):
        rows_in, (q_ref, e_ref) = refs[: len(starts)], refs[len(starts) :]
        gain = gain_ref[...]
        for (shift, offset), x_ref in zip(starts, rows_in):
            x = x_ref[...]
            base = pl.multiple_of(lax.rem(head_ref[0] + shift, HEADS) * SPAN + offset, BLK)
            n = norm(x.astype(F32), gain)
            q_ref[pl.ds(base, BLK), :] = mm_nt(n, w_ref[0]).astype(BF)
            e_ref[:, pl.ds(base, BLK)] = mm_nt(pick_ref[...], x).astype(BF)

    return body


def queries(head, gain, w, pick_cols, rows_in, starts):
    return pl.pallas_call(
        make_query_body(starts),
        out_shape=(
            jax.ShapeDtypeStruct((HEADS * SPAN, FW), BF),
            jax.ShapeDtypeStruct((FW, HEADS * SPAN), BF),
        ),
        in_specs=[SMEM] + [VMEM] * (3 + len(rows_in)),
        out_specs=[VMEM] * 2,
        compiler_params=PARAMS,
        name="fast_query",
    )(head, gain, w, pick_cols, *rows_in)


def sum_body(x_ref, o_ref):
    total = x_ref[0].astype(F32)
    for i in range(1, SEQ):
        total = total + x_ref[i].astype(F32)
    total = total.astype(BF)
    for i in range(SEQ):
        o_ref[i] = total


def sum_pieces(x):
    return pl.pallas_call(
        sum_body,
        out_shape=jax.ShapeDtypeStruct(x.shape, BF),
        in_specs=[VMEM],
        out_specs=VMEM,
        compiler_params=PARAMS,
        name="sum_pieces",
    )(x)


def renorm(updated, initial, axis):
    target = jnp.sqrt(jnp.sum(initial * initial, axis=axis, keepdims=True))
    return updated * target * lax.rsqrt(jnp.sum(updated * updated, axis=axis, keepdims=True) + EPSILON)


def apply_body(g_ref, gu_ref, down_ref, q_ref, e_ref, o_ref, gs, ws):
    for i in range(3):
        for t in range(LT):
            gs[i, :, pl.ds(t * 128, 128)] = (
                g_ref[pl.ds((i * LT + t) * 24, 24)].astype(F32).reshape(FW, 128)
            )
        init = down_ref[...] if i == 2 else gu_ref[i]
        ws[i] = renorm(init - gs[i], init, 0 if i == 2 else 1).astype(BF)
    for c in range(HEADS):
        rows = slice(c * SPAN, (c + 1) * SPAN)
        q = q_ref[rows, :]
        gate = mm(q, ws[0])
        hidden = (gate * jax.nn.sigmoid(gate) * mm(q, ws[1])).astype(BF)
        o_ref[:, rows] = (e_ref[:, rows].astype(F32) + mm_nt(ws[2], hidden)).astype(BF)


def apply(grads, gate_up, down, q, e):
    return pl.pallas_call(
        apply_body,
        out_shape=jax.ShapeDtypeStruct((FW, HEADS * SPAN), BF),
        in_specs=[VMEM] * 5,
        out_specs=VMEM,
        scratch_shapes=[pltpu.VMEM((3, FW, FH), F32), pltpu.VMEM((3, FW, FH), BF)],
        compiler_params=PARAMS,
        name="apply_fast",
    )(grads, gate_up, down, q, e)


def exchange(x, axes):
    return lax.all_to_all(x, axes, split_axis=0, concat_axis=0, tiled=True)


def shifted(x, by):
    return lax.ppermute(x, "head", [(i, (i + by) % HEADS) for i in range(HEADS)])


def on_device(
    patches,
    slot_image,
    slot_dest,
    enc_gain,
    w_qkv,
    w_out,
    fast_gain,
    w_fast,
    w_rate,
    fast_gate_up,
    fast_down,
):
    head = lax.axis_index("head")
    core = lax.axis_index("core")
    seq = lax.axis_index(SEQ_AXES)

    qkv_rows = jnp.transpose(w_qkv, (0, 2, 1)).reshape(3 * FW, D)
    half = jnp.concatenate(
        [
            lax.dynamic_slice_in_dim(qkv_rows, core * 3 * 96, 3 * 96, 0),
            lax.dynamic_slice_in_dim(w_out, core * 96, 96, 0),
        ],
        axis=0,
    )
    weights = lax.all_gather(half, ("core", "head"), axis=0, tiled=False)
    weights = weights.reshape(2, HEADS, FH, D)

    where = jnp.stack([head // 2, head % 2]).astype(jnp.int32)
    ids = jnp.stack([slot_dest, slot_image]).astype(BF)
    tile = jnp.zeros((8, 128), BF).at[:2, :16].set(ids)
    pieces = exchange(spread(where, patches.reshape(-1, 8, D), tile), SEQ_AXES)

    ids_all = pieces[:, PAIRS * LT, :2, :16].astype(jnp.int32)
    first = ids_all[:, 0, 0::2].reshape(-1)
    mine = exchange(pick(first, pieces), ALL_AXES)

    same = (ids_all[:, 1, 0::2] == ids_all[:, 1, 1::2]).reshape(-1)
    here = (first // 2 == seq * HEADS + head) & (first >= 0)
    flags = jnp.stack(
        [jnp.sum(jnp.where(here, first % 2, 0)), jnp.sum(jnp.where(here & same, 1, 0))]
    ).astype(jnp.int32)

    own_0, q1, k, v, rest = encode_first(
        flags, mine.reshape(SEQ, 4, LT, 8, 128), enc_gain.reshape(1, D), weights
    )
    before_0, after_0 = shifted(own_0, 1), shifted(own_0, -1)
    own_1 = encode_second(flags, q1, k, v, rest, weights)
    before_1, after_1 = shifted(own_1, 1), shifted(own_1, -1)
    far_0 = shifted(before_0, 1)
    far_1 = shifted(after_1, -1)

    gain = fast_gain.reshape(1, D)
    w = jnp.transpose(w_fast, (0, 2, 1))
    gate_up = fast_gate_up[0]
    down = fast_down[0].T
    shared = (gain, w, jnp.broadcast_to(w_rate.T, (FW, D)), gate_up, down)
    sums = fast((own_0, own_1), shared, None, False)
    sums = fast((before_0, after_0), shared, sums, False)
    sums = fast((before_1, after_1), shared, sums, False)
    grads = fast((far_0, far_1), shared, sums, True)

    pick_cols = (head * FW + jnp.arange(FW)[:, None] == jnp.arange(D)[None, :]).astype(BF)
    starts = ((0, 0), (0, BLK), (3, 0), (3, BLK), (1, 0), (1, BLK), (2, 0), (2, BLK))
    chunks = (own_0, own_1, before_0, before_1, after_0, after_1, far_0, far_1)
    q, e = queries(head.astype(jnp.int32).reshape(1), gain, w, pick_cols, chunks, starts)

    summed = sum_pieces(exchange(grads, SEQ_AXES).reshape(SEQ, GT // SEQ, 8, 128))
    whole = exchange(summed, SEQ_AXES).reshape(GT, 8, 128)
    return apply(whole, gate_up, down, q, e).T


def solution(mesh):
    fine = Mesh(mesh.devices.reshape(4, 4, 2, HEADS), ALL_AXES)
    in_specs = (
        P(SEQ_AXES, None),
        P(SEQ_AXES),
        P(SEQ_AXES),
        P(),
        P(None, None, "head"),
        P("head", None),
        P(),
        P(None, None, "head"),
        P(None, "head"),
        P("head", None, None, None),
        P("head", None, None),
    )
    return jax.shard_map(
        on_device, mesh=fine, in_specs=in_specs, out_specs=P(SEQ_AXES, "head"), check_vma=False
    )
```

```python
import jax
import jax.numpy as jnp
from jax import lax
from jax.experimental import pallas as pl
from jax.experimental.pallas import tpu as pltpu
from jax.sharding import Mesh, PartitionSpec as P

D = 768
HDIM = 64
BLK = 256
SPAN = 512
FW = 192
FH = 384
SEQ = 32
HEADS = 4
PAIRS = 8
LT = 3
GT = 224
WROWS = 688
KV_AT = 384
RATE_AT = 576
Q_AT = 592
EPSILON = 1e-06
LOG2E = 1.4426950408889634
RATE_SCALE = 0.1
VTOKENS = 65536
BF = jnp.bfloat16
F32 = jnp.float32
SEQ_AXES = ("x", "z", "core")
ALL_AXES = ("x", "z", "core", "head")


def params(mib):
    return pltpu.CompilerParams(vmem_limit_bytes=mib << 20)


def cost(us):
    return pl.CostEstimate(flops=0, bytes_accessed=int(us * 3.6e6), transcendentals=0)


ANY = pl.BlockSpec(memory_space=pltpu.HBM)
SMEM = pl.BlockSpec(memory_space=pltpu.SMEM)
VMEM = pl.BlockSpec(memory_space=pltpu.VMEM)


def in_hbm(x):
    return pltpu.with_memory_space_constraint(x, pltpu.HBM)


def mm(a, b):
    return jnp.dot(a, b, preferred_element_type=F32)


def mm_nt(a, b):
    return lax.dot_general(a, b, (((1,), (1,)), ((), ())), preferred_element_type=F32)


def mm_tn(a, b):
    return lax.dot_general(a, b, (((0,), (0,)), ((), ())), preferred_element_type=F32)


def norm(rows, gain):
    factor = lax.rsqrt(jnp.mean(rows * rows, axis=-1, keepdims=True) + EPSILON)
    return (rows * factor * gain).astype(BF)


def spread_body(
    at_ref, x_ref, meta_ref, qkv_ref, out_ref, fast_ref, rate_ref,
    o_ref, w_ref, buf, sems, wsems,
):
    head = at_ref[1]
    core = at_ref[2]
    parity = head // 2
    half = head % 2
    copies = []
    for p in range(PAIRS):
        copies.append(
            pltpu.make_async_copy(
                x_ref.at[
                    pl.ds(p * 64 + parity * 32, SEQ), :, pl.ds(pl.multiple_of(half * FH, 128), FH)
                ],
                buf.at[p],
                sems.at[p],
            )
        )
        copies[p].start()

    def rows(ref, start, count):
        return ref.at[pl.ds(pl.multiple_of(start, 32), count)]

    moves = [
        (rows(qkv_ref, core * 288, 288), w_ref.at[pl.ds(0, 288)]),
        (rows(out_ref, core * 96, 96), w_ref.at[pl.ds(288, 96)]),
        (rows(fast_ref, FW + core * FW, FW), w_ref.at[pl.ds(KV_AT, FW)]),
        (rate_ref, w_ref.at[pl.ds(RATE_AT, 16)]),
        (rows(fast_ref, core * 96, 96), w_ref.at[pl.ds(Q_AT, 96)]),
    ]
    moves = [pltpu.make_async_copy(*m, wsems.at[i]) for i, m in enumerate(moves)]
    for m in moves:
        m.start()
    o_ref[:, PAIRS * LT] = jnp.broadcast_to(meta_ref[...][None], (SEQ, 8, 128))
    for p in range(PAIRS):
        copies[p].wait()
        for t in range(LT):
            o_ref[:, p * LT + t] = buf[p, :, :, t * 128 : (t + 1) * 128]
    for m in moves:
        m.wait()


def spread(at, x, meta, *weights):
    return pl.pallas_call(
        spread_body,
        out_shape=(
            jax.ShapeDtypeStruct((SEQ, PAIRS * LT + 1, 8, 128), BF),
            jax.ShapeDtypeStruct((WROWS, D), BF),
        ),
        in_specs=[SMEM, ANY, VMEM] + [ANY] * 4,
        out_specs=[VMEM] * 2,
        scratch_shapes=[
            pltpu.VMEM((PAIRS, SEQ, 8, FH), BF),
            pltpu.SemaphoreType.DMA((PAIRS,)),
            pltpu.SemaphoreType.DMA((5,)),
        ],
        compiler_params=params(12),
        cost_estimate=cost(3),
        name="spread",
    )(at, in_hbm(x), meta, *[in_hbm(w) for w in weights])


def pick_body(at_ref, x_ref, o_ref, flag_ref, ids, table, source, sem):
    ids[...] = x_ref[:, PAIRS * LT, 0, :].astype(F32).astype(jnp.int32)
    copy = pltpu.make_async_copy(ids, table, sem)
    copy.start()
    copy.wait()

    def note(q, carry):
        first = table[q // PAIRS, (q % PAIRS) * 2]
        pair = jnp.minimum(first // 2, SEQ * HEADS - 1)
        source[jnp.where(first >= 0, pair, SEQ * HEADS)] = q
        return carry

    lax.fori_loop(0, SEQ * PAIRS, note, 0, unroll=8)

    def move(m, carry):
        q = source[m]
        o_ref[m] = x_ref[q // PAIRS, pl.ds((q % PAIRS) * LT, LT)]
        return carry

    lax.fori_loop(0, SEQ * HEADS, move, 0, unroll=8)
    q = source[at_ref[0]]
    slot = (q % PAIRS) * 2
    flag_ref[0] = table[q // PAIRS, slot] % 2
    flag_ref[1] = jnp.where(
        table[q // PAIRS, 16 + slot] == table[q // PAIRS, 17 + slot], 1, 0
    )
    flag_ref[2] = at_ref[1]


def pick(at, x):
    return pl.pallas_call(
        pick_body,
        out_shape=(
            jax.ShapeDtypeStruct((SEQ * HEADS, LT, 8, 128), BF),
            jax.ShapeDtypeStruct((3,), jnp.int32),
        ),
        in_specs=[SMEM, VMEM],
        out_specs=[VMEM, SMEM],
        scratch_shapes=[
            pltpu.VMEM((SEQ, 128), jnp.int32),
            pltpu.SMEM((SEQ, 128), jnp.int32),
            pltpu.SMEM((SEQ * HEADS + 8,), jnp.int32),
            pltpu.SemaphoreType.DMA(()),
        ],
        compiler_params=params(8),
        cost_estimate=cost(3),
        name="pick",
    )(at, x)


def attend(block, bias, q, k, v):
    lane = lax.broadcasted_iota(jnp.int32, (BLK, FW), 1)
    out = None
    for j in range(FW // HDIM):
        mine = (lane >= j * HDIM) & (lane < (j + 1) * HDIM)
        s = mm_nt(jnp.where(mine, q, jnp.zeros_like(q)), k)
        parts = [s[:, :BLK], s[:, BLK:]]
        parts[1 - block] = parts[1 - block] + bias
        top = jnp.max(jnp.maximum(parts[0], parts[1]), axis=-1, keepdims=True)
        p = jnp.concatenate([jnp.exp2(x - top).astype(BF) for x in parts], axis=1)
        o = mm(p, v)
        o = o[:, :FW] * (1.0 / o[:, FW : FW + 1])
        out = o if out is None else jnp.where(mine, o, out)
    return out.astype(BF)


def key_copies(head, w_ref, fs, sems):
    return [
        pltpu.make_async_copy(
            w_ref.at[:, lax.rem(head + d, HEADS), pl.ds(KV_AT, FW + 16)], fs.at[d], sems.at[d]
        )
        for d in range(HEADS)
    ]


def project(block, gain, copies, fs, kv_refs):
    n = norm(block.astype(F32), gain)
    lane = lax.broadcasted_iota(jnp.int32, (BLK, 2 * FW), 1)
    for c in copies:
        c.wait()
    z = mm_nt(n, jnp.concatenate([fs[d, 0, FW:] for d in range(HEADS)], axis=0))
    soft = jnp.maximum(z, 0.0) + jnp.log1p(jnp.exp(-jnp.abs(z)))
    rates = -(RATE_SCALE * VTOKENS**-0.5) * soft
    for d, kv_ref in enumerate(kv_refs):
        kv = mm_nt(n, fs[d, :, :FW].reshape(2 * FW, D)).astype(BF).astype(F32)
        kv_ref[...] = jnp.where(lane < FW, kv, kv * rates[:, d * 16 : d * 16 + 1]).astype(BF)


def encode_first_body(
    flag_ref, x_ref, gain_ref, fgain_ref, w_ref,
    o_ref, kv0, kv1, kv2, kv3, q_ref, k_ref, v_ref, rest_ref,
    xs, ns, ws, fs, sems, fsems,
):
    copies = [
        pltpu.make_async_copy(w_ref.at[:, g, pl.ds(0, FH)], ws.at[g], sems.at[g])
        for g in range(HEADS)
    ]
    later = key_copies(flag_ref[2], w_ref, fs, fsems)
    for c in copies + later:
        c.start()
    flip = flag_ref[0]
    bias = jnp.where(flag_ref[1] != 0, 0.0, -1e30).astype(F32)
    for b in range(2):
        base = pl.multiple_of(jnp.bitwise_xor(flip, b) * BLK, BLK)
        for c in range(2):
            for t in range(LT):
                xs[pl.ds(base, BLK), pl.ds(c * FH + t * 128, 128)] = (
                    x_ref[:, 2 * b + c, t].astype(F32).reshape(BLK, 128)
                )
    gain = gain_ref[...]
    for r in range(8):
        ns[pl.ds(r * 64, 64), :] = norm(xs[pl.ds(r * 64, 64), :], gain)
    rest_ref[...] = xs[BLK:, :].astype(BF)
    n = ns[...]
    scale = HDIM**-0.5 * LOG2E
    out = xs[:BLK, :]
    for g in range(HEADS):
        copies[g].wait()
        w = ws[g, :, : 3 * 96].reshape(3 * FW, D)
        q = (mm_nt(n, w[:FW]) * scale).astype(BF)
        k = mm_nt(n, w[FW : 2 * FW]).astype(BF)
        v = jnp.concatenate(
            [mm_nt(n, w[2 * FW :]).astype(BF), jnp.ones((SPAN, HDIM), BF)], axis=1
        )
        q_ref[g] = q[BLK:]
        k_ref[g] = k
        v_ref[g] = v
        att = attend(0, bias, q[:BLK], k, v)
        out = out + mm(att, ws[g, :, 3 * 96 :].reshape(FW, D))
    out = out.astype(BF)
    o_ref[...] = out
    project(out, fgain_ref[...], later, fs, (kv0, kv1, kv2, kv3))


def encode_first(flags, x, gain, fgain, w):
    return pl.pallas_call(
        encode_first_body,
        out_shape=(
            jax.ShapeDtypeStruct((BLK, D), BF),
            *[jax.ShapeDtypeStruct((BLK, 2 * FW), BF)] * HEADS,
            jax.ShapeDtypeStruct((HEADS, BLK, FW), BF),
            jax.ShapeDtypeStruct((HEADS, SPAN, FW), BF),
            jax.ShapeDtypeStruct((HEADS, SPAN, FW + HDIM), BF),
            jax.ShapeDtypeStruct((BLK, D), BF),
        ),
        in_specs=[SMEM, VMEM, VMEM, VMEM, ANY],
        out_specs=[VMEM] * 9,
        scratch_shapes=[
            pltpu.VMEM((SPAN, D), F32),
            pltpu.VMEM((SPAN, D), BF),
            pltpu.VMEM((HEADS, 2, FH, D), BF),
            pltpu.VMEM((HEADS, 2, FW + 16, D), BF),
            pltpu.SemaphoreType.DMA((HEADS,)),
            pltpu.SemaphoreType.DMA((HEADS,)),
        ],
        compiler_params=params(24),
        cost_estimate=cost(9),
        name="encode_first",
    )(flags, x, gain, fgain, w)


def encode_second_body(
    flag_ref, fgain_ref, q_ref, k_ref, v_ref, rest_ref, w_ref,
    o_ref, kv0, kv1, kv2, kv3, ws, fs, sem, fsems,
):
    copy = pltpu.make_async_copy(w_ref.at[:, :, pl.ds(3 * 96, 96)], ws, sem)
    copy.start()
    later = key_copies(flag_ref[2], w_ref, fs, fsems)
    for c in later:
        c.start()
    bias = jnp.where(flag_ref[1] != 0, 0.0, -1e30).astype(F32)
    out = rest_ref[...].astype(F32)
    for g in range(HEADS):
        att = attend(1, bias, q_ref[g], k_ref[g], v_ref[g])
        if g == 0:
            copy.wait()
        out = out + mm(att, ws[:, g].reshape(FW, D))
    out = out.astype(BF)
    o_ref[...] = out
    project(out, fgain_ref[...], later, fs, (kv0, kv1, kv2, kv3))


def encode_second(flags, fgain, q, k, v, rest, w):
    return pl.pallas_call(
        encode_second_body,
        out_shape=(
            jax.ShapeDtypeStruct((BLK, D), BF),
            *[jax.ShapeDtypeStruct((BLK, 2 * FW), BF)] * HEADS,
        ),
        in_specs=[SMEM, VMEM, VMEM, VMEM, VMEM, VMEM, ANY],
        out_specs=[VMEM] * 5,
        scratch_shapes=[
            pltpu.VMEM((2, HEADS, 96, D), BF),
            pltpu.VMEM((HEADS, 2, FW + 16, D), BF),
            pltpu.SemaphoreType.DMA(()),
            pltpu.SemaphoreType.DMA((HEADS,)),
        ],
        compiler_params=params(16),
        cost_estimate=cost(20),
        name="encode_second",
    )(flags, fgain, q, k, v, rest, w)


def query_body(flag_ref, x0_ref, x1_ref, gain_ref, w_ref, *refs):
    own_ref, up_ref, down_ref, ws, sems = refs
    whole = {0: own_ref, 1: up_ref, 3: down_ref}
    head = flag_ref[2]
    copies = [
        pltpu.make_async_copy(
            w_ref.at[:, lax.rem(head + d, HEADS), pl.ds(Q_AT, 96)], ws.at[d], sems.at[d]
        )
        for d in range(HEADS)
    ]
    for c in copies:
        c.start()
    xs = (x0_ref[...], x1_ref[...])
    ns = [norm(x.astype(F32), gain_ref[...]) for x in xs]
    cols = [[x[:, g * FW : (g + 1) * FW] for g in range(HEADS)] for x in xs]
    for d in range(HEADS):
        there = lax.rem(head + d, HEADS)
        copies[d].wait()
        w = ws[d].reshape(FW, D)
        for i in range(2):
            q = mm_nt(ns[i], w).astype(BF)
            c = cols[i]
            e = jnp.where(
                there < 2, jnp.where(there == 0, c[0], c[1]), jnp.where(there == 2, c[2], c[3])
            )
            qe = jnp.concatenate([q, e], axis=1)
            if d == 2:
                (up_ref, down_ref)[i][SPAN:, :] = qe
            else:
                whole[d][pl.ds(i * BLK, BLK), :] = qe


def query(flags, x0, x1, gain, w):
    return pl.pallas_call(
        query_body,
        out_shape=(
            jax.ShapeDtypeStruct((SPAN, 2 * FW), BF),
            jax.ShapeDtypeStruct((SPAN + BLK, 2 * FW), BF),
            jax.ShapeDtypeStruct((SPAN + BLK, 2 * FW), BF),
        ),
        in_specs=[SMEM, VMEM, VMEM, VMEM, ANY],
        out_specs=[VMEM] * 3,
        scratch_shapes=[
            pltpu.VMEM((HEADS, 2, 96, D), BF),
            pltpu.SemaphoreType.DMA((HEADS,)),
        ],
        compiler_params=params(12),
        cost_estimate=cost(4),
        name="fast_query",
    )(flags, x0, x1, gain, w)


def make_fast_body(blocks, first, last):
    def body(*refs):
        kv_refs = refs[:blocks]
        gu_ref, down_ref = refs[blocks : blocks + 2]
        sum_ref = None if first else refs[blocks + 2]
        g_ref = refs[-1]
        gate_up = [gu_ref[i].astype(BF) for i in range(2)]
        down = down_ref[...].astype(BF)
        sums = None
        for kv_ref in kv_refs:
            key = kv_ref[:, :FW]
            out_grad = kv_ref[:, FW:]
            gate = mm(key, gate_up[0])
            up = mm(key, gate_up[1])
            hidden_grad = mm(out_grad, down)
            s = jax.nn.sigmoid(gate)
            silu = gate * s
            hidden = (silu * up).astype(BF)
            gate_grad = (hidden_grad * up * s * (1.0 + gate * (1.0 - s))).astype(BF)
            up_grad = (hidden_grad * silu).astype(BF)
            parts = [mm_tn(key, gate_grad), mm_tn(key, up_grad), mm_tn(out_grad, hidden)]
            sums = parts if sums is None else [a + b for a, b in zip(sums, parts)]
        for i, total in enumerate(sums):
            if not first:
                total = total + sum_ref[i]
            if last:
                for t in range(LT):
                    g_ref[pl.ds((i * LT + t) * 24, 24)] = (
                        total[:, t * 128 : (t + 1) * 128].astype(BF).reshape(24, 8, 128)
                    )
            else:
                g_ref[i] = total
        if last:
            g_ref[pl.ds(216, 8)] = jnp.zeros((8, 8, 128), BF)

    return body


def fast(blocks, shared, sums, last):
    first = sums is None
    operands = (*blocks, *shared) + (() if first else (sums,))
    return pl.pallas_call(
        make_fast_body(len(blocks), first, last),
        out_shape=(
            jax.ShapeDtypeStruct((GT, 8, 128), BF)
            if last
            else jax.ShapeDtypeStruct((3, FW, FH), F32)
        ),
        in_specs=[VMEM] * len(operands),
        out_specs=VMEM,
        compiler_params=params(16),
        cost_estimate=cost(3),
        name="fast_grad",
    )(*operands)


def sum_body(x_ref, o_ref):
    total = x_ref[0].astype(F32)
    for i in range(1, SEQ):
        total = total + x_ref[i].astype(F32)
    total = total.astype(BF)
    for i in range(SEQ):
        o_ref[i] = total


def sum_pieces(x):
    return pl.pallas_call(
        sum_body,
        out_shape=jax.ShapeDtypeStruct(x.shape, BF),
        in_specs=[VMEM],
        out_specs=VMEM,
        compiler_params=params(4),
        cost_estimate=cost(1),
        name="sum_pieces",
    )(x)


def renorm(updated, initial, axis):
    target = jnp.sqrt(jnp.sum(initial * initial, axis=axis, keepdims=True))
    return updated * target * lax.rsqrt(jnp.sum(updated * updated, axis=axis, keepdims=True) + EPSILON)


def apply_body(head_ref, g_ref, gu_ref, down_ref, *refs):
    qe_refs, (o_ref, gs, ws) = refs[:5], refs[5:]
    for i in range(3):
        for t in range(LT):
            gs[i, :, pl.ds(t * 128, 128)] = (
                g_ref[pl.ds((i * LT + t) * 24, 24)].astype(F32).reshape(FW, 128)
            )
        init = down_ref[...] if i == 2 else gu_ref[i]
        ws[i] = renorm(init - gs[i], init, 0 if i == 2 else 1).astype(BF)
    row = lax.broadcasted_iota(jnp.int32, (FW, 2 * FW), 0)
    col = lax.broadcasted_iota(jnp.int32, (FW, 2 * FW), 1)
    columns = jnp.where(row + FW == col, 1.0, 0.0).astype(BF)
    own_ref, up_ref, down_side_ref, far0_ref, far1_ref = qe_refs
    for d in range(HEADS):
        if d == 2:
            qe = jnp.concatenate([far0_ref[...], far1_ref[...]], axis=0)
        else:
            qe = {0: own_ref, 1: up_ref, 3: down_side_ref}[d][:SPAN, :]
        q = qe[:, :FW]
        gate = mm(q, ws[0])
        hidden = (gate * jax.nn.sigmoid(gate) * mm(q, ws[1])).astype(BF)
        base = pl.multiple_of(lax.rem(head_ref[2] + HEADS - d, HEADS) * SPAN, SPAN)
        o_ref[:, pl.ds(base, SPAN)] = (mm_nt(columns, qe) + mm_nt(ws[2], hidden)).astype(BF)


def apply(flags, grads, gate_up, down, qes):
    return pl.pallas_call(
        apply_body,
        out_shape=jax.ShapeDtypeStruct((FW, HEADS * SPAN), BF),
        in_specs=[SMEM] + [VMEM] * 8,
        out_specs=VMEM,
        scratch_shapes=[pltpu.VMEM((3, FW, FH), F32), pltpu.VMEM((3, FW, FH), BF)],
        compiler_params=params(16),
        cost_estimate=cost(3),
        name="apply_fast",
    )(flags, grads, gate_up, down, *qes)


def exchange(x, axes):
    return lax.all_to_all(x, axes, split_axis=0, concat_axis=0, tiled=True)


def shifted(x, by):
    return lax.ppermute(x, "head", [(i, (i + by) % HEADS) for i in range(HEADS)])


def on_device(
    patches,
    slot_image,
    slot_dest,
    enc_gain,
    w_qkv,
    w_out,
    fast_gain,
    w_fast,
    w_rate,
    fast_gate_up,
    fast_down,
):
    head = lax.axis_index("head")
    core = lax.axis_index("core")
    seq = lax.axis_index(SEQ_AXES)
    at = jnp.stack([seq * HEADS + head, head, core]).astype(jnp.int32)

    ids = jnp.concatenate([slot_dest, slot_image]).astype(BF)
    tile = jnp.pad(ids[None, :], ((0, 7), (0, 96)))
    pieces, rows = spread(
        at,
        patches.reshape(-1, 8, D),
        tile,
        jnp.transpose(w_qkv, (0, 2, 1)).reshape(3 * FW, D),
        w_out,
        jnp.transpose(w_fast, (0, 2, 1)).reshape(3 * FW, D),
        jnp.broadcast_to(w_rate.T, (16, D)),
    )
    weights = lax.all_gather(rows, ("core", "head"), axis=0, tiled=False)
    weights = in_hbm(weights.reshape(2, HEADS, WROWS, D))
    picked, flags = pick(at, exchange(pieces, SEQ_AXES))
    mine = exchange(picked, ALL_AXES)

    fgain = fast_gain.reshape(1, D)
    own_0, *outs = encode_first(
        flags, mine.reshape(SEQ, 4, LT, 8, 128), enc_gain.reshape(1, D), fgain, weights
    )
    kv_0, carried = tuple(outs[:HEADS]), outs[HEADS:]
    got_0 = tuple(shifted(kv_0[d], d) for d in range(1, HEADS))
    own_1, *kv_1 = encode_second(flags, fgain, *carried, weights)
    kv_1 = tuple(kv_1)
    kv_1, got_0 = lax.optimization_barrier((kv_1, got_0))
    got_1 = tuple(shifted(kv_1[d], d) for d in range(1, HEADS))

    gate_up = fast_gate_up[0]
    down = fast_down[0].T
    sums = fast((kv_0[0], kv_1[0]), (gate_up, down), None, False)
    sums = fast(got_0, (gate_up, down), sums, False)
    qe = query(flags, own_0, own_1, fgain, weights)
    got_1, qe = lax.optimization_barrier((got_1, tuple(qe)))
    grads = fast(got_1, (gate_up, down), sums, True)

    own_qe, up_qe, down_qe = qe
    up_qe, down_qe = shifted(up_qe, 1), shifted(down_qe, -1)
    far_qe = (shifted(up_qe[SPAN:], 1), shifted(down_qe[SPAN:], -1))
    arrived = exchange(grads, SEQ_AXES)
    whole = exchange(sum_pieces(arrived.reshape(SEQ, GT // SEQ, 8, 128)), SEQ_AXES)
    return apply(
        flags,
        whole.reshape(GT, 8, 128),
        gate_up,
        down,
        (own_qe, up_qe, down_qe, *far_qe),
    ).T


def solution(mesh):
    fine = Mesh(mesh.devices.reshape(4, 4, 2, HEADS), ALL_AXES)
    in_specs = (
        P(SEQ_AXES, None),
        P(SEQ_AXES),
        P(SEQ_AXES),
        P(),
        P(None, None, "head"),
        P("head", None),
        P(),
        P(None, None, "head"),
        P(None, "head"),
        P("head", None, None, None),
        P("head", None, None),
    )
    return jax.shard_map(
        on_device, mesh=fine, in_specs=in_specs, out_specs=P(SEQ_AXES, "head"), check_vma=False
    )
```

```python
import jax
import jax.numpy as jnp
from jax import lax
from jax.experimental import pallas as pl
from jax.experimental.pallas import tpu as pltpu
from jax.sharding import Mesh, PartitionSpec as P

D = 768
HDIM = 64
BLK = 256
SPAN = 512
FW = 192
FH = 384
SEQ = 32
HEADS = 4
PAIRS = 8
LT = 3
GT = 224
WROWS = 688
KV_AT = 384
RATE_AT = 576
Q_AT = 592
CUT = 352
EPSILON = 1e-06
LOG2E = 1.4426950408889634
RATE_SCALE = 0.1
VTOKENS = 65536
BF = jnp.bfloat16
F32 = jnp.float32
SEQ_AXES = ("x", "z", "core")
ALL_AXES = ("x", "z", "core", "head")


def params(mib):
    return pltpu.CompilerParams(vmem_limit_bytes=mib << 20)


def cost(us):
    return pl.CostEstimate(flops=0, bytes_accessed=int(us * 3.6e6), transcendentals=0)


ANY = pl.BlockSpec(memory_space=pltpu.HBM)
SMEM = pl.BlockSpec(memory_space=pltpu.SMEM)
VMEM = pl.BlockSpec(memory_space=pltpu.VMEM)


def in_hbm(x):
    return pltpu.with_memory_space_constraint(x, pltpu.HBM)


def mm(a, b):
    return jnp.dot(a, b, preferred_element_type=F32)


def mm_nt(a, b):
    return lax.dot_general(a, b, (((1,), (1,)), ((), ())), preferred_element_type=F32)


def mm_tn(a, b):
    return lax.dot_general(a, b, (((0,), (0,)), ((), ())), preferred_element_type=F32)


def norm(rows, gain):
    factor = lax.rsqrt(jnp.mean(rows * rows, axis=-1, keepdims=True) + EPSILON)
    return (rows * factor * gain).astype(BF)


def spread_body(
    at_ref, x_ref, meta_ref, qkv_ref, out_ref, fast_ref, rate_ref,
    o_ref, low_ref, high_ref, buf, w_ref, sems, wsems, osem,
):
    head = at_ref[1]
    core = at_ref[2]
    parity = head // 2
    half = head % 2
    copies = []
    for p in range(PAIRS):
        copies.append(
            pltpu.make_async_copy(
                x_ref.at[
                    pl.ds(p * 64 + parity * 32, SEQ), :, pl.ds(pl.multiple_of(half * FH, 128), FH)
                ],
                buf.at[p],
                sems.at[p],
            )
        )
        copies[p].start()

    def rows(ref, start, count):
        return ref.at[pl.ds(pl.multiple_of(start, 32), count)]

    moves = [
        (rows(qkv_ref, core * 288, 288), w_ref.at[pl.ds(0, 288)]),
        (rows(out_ref, core * 96, 96), w_ref.at[pl.ds(288, 96)]),
        (rows(fast_ref, FW + core * FW, FW), w_ref.at[pl.ds(KV_AT, FW)]),
        (rate_ref, w_ref.at[pl.ds(RATE_AT, 16)]),
        (rows(fast_ref, core * 96, 96), w_ref.at[pl.ds(Q_AT, 96)]),
    ]
    moves = [pltpu.make_async_copy(*m, wsems.at[i]) for i, m in enumerate(moves)]
    for m in moves:
        m.start()
    o_ref[:, PAIRS * LT] = jnp.broadcast_to(meta_ref[...][None], (SEQ, 8, 128))
    for m in moves:
        m.wait()
    outs = [
        pltpu.make_async_copy(w_ref.at[pl.ds(0, CUT)], low_ref, osem.at[0]),
        pltpu.make_async_copy(w_ref.at[pl.ds(CUT, WROWS - CUT)], high_ref, osem.at[1]),
    ]
    for c in outs:
        c.start()
    for p in range(PAIRS):
        copies[p].wait()
        for t in range(LT):
            o_ref[:, p * LT + t] = buf[p, :, :, t * 128 : (t + 1) * 128]
    for c in outs:
        c.wait()


def spread(at, x, meta, *weights):
    return pl.pallas_call(
        spread_body,
        out_shape=(
            jax.ShapeDtypeStruct((SEQ, PAIRS * LT + 1, 8, 128), BF),
            pltpu.HBM((CUT, D), BF),
            pltpu.HBM((WROWS - CUT, D), BF),
        ),
        in_specs=[SMEM, ANY, VMEM] + [ANY] * 4,
        out_specs=[VMEM, ANY, ANY],
        scratch_shapes=[
            pltpu.VMEM((PAIRS, SEQ, 8, FH), BF),
            pltpu.VMEM((WROWS, D), BF),
            pltpu.SemaphoreType.DMA((PAIRS,)),
            pltpu.SemaphoreType.DMA((5,)),
            pltpu.SemaphoreType.DMA((2,)),
        ],
        compiler_params=params(12),
        cost_estimate=cost(3),
        name="spread",
    )(at, in_hbm(x), meta, *[in_hbm(w) for w in weights])


def pick_body(at_ref, x_ref, o_ref, flag_ref, ids, table, source, sem):
    ids[...] = x_ref[:, PAIRS * LT, 0, :].astype(F32).astype(jnp.int32)
    copy = pltpu.make_async_copy(ids, table, sem)
    copy.start()
    copy.wait()

    def note(q, carry):
        first = table[q // PAIRS, (q % PAIRS) * 2]
        pair = jnp.minimum(first // 2, SEQ * HEADS - 1)
        source[jnp.where(first >= 0, pair, SEQ * HEADS)] = q
        return carry

    lax.fori_loop(0, SEQ * PAIRS, note, 0, unroll=8)

    def move(m, carry):
        q = source[m]
        o_ref[m] = x_ref[q // PAIRS, pl.ds((q % PAIRS) * LT, LT)]
        return carry

    lax.fori_loop(0, SEQ * HEADS, move, 0, unroll=8)
    q = source[at_ref[0]]
    slot = (q % PAIRS) * 2
    flag_ref[0] = table[q // PAIRS, slot] % 2
    flag_ref[1] = jnp.where(
        table[q // PAIRS, 16 + slot] == table[q // PAIRS, 17 + slot], 1, 0
    )
    flag_ref[2] = at_ref[1]
    flag_ref[3] = at_ref[2]


def pick(at, x):
    return pl.pallas_call(
        pick_body,
        out_shape=(
            jax.ShapeDtypeStruct((SEQ * HEADS, LT, 8, 128), BF),
            jax.ShapeDtypeStruct((4,), jnp.int32),
        ),
        in_specs=[SMEM, VMEM],
        out_specs=[VMEM, SMEM],
        scratch_shapes=[
            pltpu.VMEM((SEQ, 128), jnp.int32),
            pltpu.SMEM((SEQ, 128), jnp.int32),
            pltpu.SMEM((SEQ * HEADS + 8,), jnp.int32),
            pltpu.SemaphoreType.DMA(()),
        ],
        compiler_params=params(8),
        cost_estimate=cost(3),
        name="pick",
    )(at, x)


def weight_copies(core, w_refs, d, start, count, dst, sem):
    copies = []
    low = max(0, min(count, CUT - start))
    for side in range(2):
        to = dst.at[core if side == 0 else 1 - core]
        low_ref, high_ref = w_refs[side * 8 + d * 2 : side * 8 + d * 2 + 2]
        pieces = [(low_ref, start, 0, low), (high_ref, start + low - CUT, low, count - low)]
        for ref, at, put, n in pieces:
            if n:
                copies.append(
                    pltpu.make_async_copy(ref.at[pl.ds(at, n)], to.at[pl.ds(put, n)], sem)
                )
    return copies


def wait_all(dst, sem):
    pltpu.make_async_copy(dst, dst, sem).wait()


def attend(block, bias, q, k, v):
    lane = lax.broadcasted_iota(jnp.int32, (BLK, FW), 1)
    out = None
    for j in range(FW // HDIM):
        mine = (lane >= j * HDIM) & (lane < (j + 1) * HDIM)
        s = mm_nt(jnp.where(mine, q, jnp.zeros_like(q)), k)
        parts = [s[:, :BLK], s[:, BLK:]]
        parts[1 - block] = parts[1 - block] + bias
        top = jnp.max(jnp.maximum(parts[0], parts[1]), axis=-1, keepdims=True)
        p = jnp.concatenate([jnp.exp2(x - top).astype(BF) for x in parts], axis=1)
        o = mm(p, v)
        o = o[:, :FW] * (1.0 / o[:, FW : FW + 1])
        out = o if out is None else jnp.where(mine, o, out)
    return out.astype(BF)


def project(block, gain, fs, fsems, kv_refs):
    n = norm(block.astype(F32), gain)
    lane = lax.broadcasted_iota(jnp.int32, (BLK, 2 * FW), 1)
    for d in range(HEADS):
        wait_all(fs.at[d], fsems.at[d])
    z = mm_nt(n, jnp.concatenate([fs[d, 0, FW:] for d in range(HEADS)], axis=0))
    soft = jnp.maximum(z, 0.0) + jnp.log1p(jnp.exp(-jnp.abs(z)))
    rates = -(RATE_SCALE * VTOKENS**-0.5) * soft
    for d, kv_ref in enumerate(kv_refs):
        kv = mm_nt(n, fs[d, :, :FW].reshape(2 * FW, D)).astype(BF).astype(F32)
        kv_ref[...] = jnp.where(lane < FW, kv, kv * rates[:, d * 16 : d * 16 + 1]).astype(BF)


def encode_first_body(
    flag_ref, x_ref, gain_ref, fgain_ref, *refs
):
    w_refs = refs[:16]
    o_ref, kv0, kv1, kv2, kv3, q_ref, k_ref, v_ref, rest_ref = refs[16:25]
    xs, ns, ws, fs, sems, fsems = refs[25:]
    core = flag_ref[3]
    for d in range(HEADS):
        for c in weight_copies(core, w_refs, d, 0, FH, ws.at[d], sems.at[d]):
            c.start()
    for d in range(HEADS):
        for c in weight_copies(core, w_refs, d, KV_AT, FW + 16, fs.at[d], fsems.at[d]):
            c.start()
    flip = flag_ref[0]
    bias = jnp.where(flag_ref[1] != 0, 0.0, -1e30).astype(F32)
    for b in range(2):
        base = pl.multiple_of(jnp.bitwise_xor(flip, b) * BLK, BLK)
        for c in range(2):
            for t in range(LT):
                xs[pl.ds(base, BLK), pl.ds(c * FH + t * 128, 128)] = (
                    x_ref[:, 2 * b + c, t].astype(F32).reshape(BLK, 128)
                )
    gain = gain_ref[...]
    for r in range(8):
        ns[pl.ds(r * 64, 64), :] = norm(xs[pl.ds(r * 64, 64), :], gain)
    rest_ref[...] = xs[BLK:, :].astype(BF)
    n = ns[...]
    scale = HDIM**-0.5 * LOG2E
    out = xs[:BLK, :]
    for g in range(HEADS):
        wait_all(ws.at[g], sems.at[g])
        w = ws[g, :, : 3 * 96].reshape(3 * FW, D)
        q = (mm_nt(n, w[:FW]) * scale).astype(BF)
        k = mm_nt(n, w[FW : 2 * FW]).astype(BF)
        v = jnp.concatenate(
            [mm_nt(n, w[2 * FW :]).astype(BF), jnp.ones((SPAN, HDIM), BF)], axis=1
        )
        q_ref[g] = q[BLK:]
        k_ref[g] = k
        v_ref[g] = v
        att = attend(0, bias, q[:BLK], k, v)
        out = out + mm(att, ws[g, :, 3 * 96 :].reshape(FW, D))
    out = out.astype(BF)
    o_ref[...] = out
    project(out, fgain_ref[...], fs, fsems, (kv0, kv1, kv2, kv3))


def encode_first(flags, x, gain, fgain, weights):
    return pl.pallas_call(
        encode_first_body,
        out_shape=(
            jax.ShapeDtypeStruct((BLK, D), BF),
            *[jax.ShapeDtypeStruct((BLK, 2 * FW), BF)] * HEADS,
            jax.ShapeDtypeStruct((HEADS, BLK, FW), BF),
            jax.ShapeDtypeStruct((HEADS, SPAN, FW), BF),
            jax.ShapeDtypeStruct((HEADS, SPAN, FW + HDIM), BF),
            jax.ShapeDtypeStruct((BLK, D), BF),
        ),
        in_specs=[SMEM, VMEM, VMEM, VMEM] + [ANY] * 16,
        out_specs=[VMEM] * 9,
        scratch_shapes=[
            pltpu.VMEM((SPAN, D), F32),
            pltpu.VMEM((SPAN, D), BF),
            pltpu.VMEM((HEADS, 2, FH, D), BF),
            pltpu.VMEM((HEADS, 2, FW + 16, D), BF),
            pltpu.SemaphoreType.DMA((HEADS,)),
            pltpu.SemaphoreType.DMA((HEADS,)),
        ],
        compiler_params=params(24),
        cost_estimate=cost(9),
        name="encode_first",
    )(flags, x, gain, fgain, *weights)


def encode_second_body(
    flag_ref, fgain_ref, q_ref, k_ref, v_ref, rest_ref, *refs
):
    w_refs = refs[:16]
    o_ref, kv0, kv1, kv2, kv3, ws, fs, sem, fsems = refs[16:]
    core = flag_ref[3]
    for d in range(HEADS):
        for c in weight_copies(core, w_refs, d, 3 * 96, 96, ws.at[d], sem):
            c.start()
    for d in range(HEADS):
        for c in weight_copies(core, w_refs, d, KV_AT, FW + 16, fs.at[d], fsems.at[d]):
            c.start()
    bias = jnp.where(flag_ref[1] != 0, 0.0, -1e30).astype(F32)
    out = rest_ref[...].astype(F32)
    for g in range(HEADS):
        att = attend(1, bias, q_ref[g], k_ref[g], v_ref[g])
        if g == 0:
            wait_all(ws, sem)
        out = out + mm(att, ws[g].reshape(FW, D))
    out = out.astype(BF)
    o_ref[...] = out
    project(out, fgain_ref[...], fs, fsems, (kv0, kv1, kv2, kv3))


def encode_second(flags, fgain, q, k, v, rest, weights):
    return pl.pallas_call(
        encode_second_body,
        out_shape=(
            jax.ShapeDtypeStruct((BLK, D), BF),
            *[jax.ShapeDtypeStruct((BLK, 2 * FW), BF)] * HEADS,
        ),
        in_specs=[SMEM] + [VMEM] * 5 + [ANY] * 16,
        out_specs=[VMEM] * 5,
        scratch_shapes=[
            pltpu.VMEM((HEADS, 2, 96, D), BF),
            pltpu.VMEM((HEADS, 2, FW + 16, D), BF),
            pltpu.SemaphoreType.DMA(()),
            pltpu.SemaphoreType.DMA((HEADS,)),
        ],
        compiler_params=params(16),
        cost_estimate=cost(20),
        name="encode_second",
    )(flags, fgain, q, k, v, rest, *weights)


def query_body(flag_ref, x0_ref, x1_ref, gain_ref, *refs):
    w_refs = refs[:16]
    own_ref, up_ref, down_ref, ws, sems = refs[16:]
    whole = {0: own_ref, 1: up_ref, 3: down_ref}
    head = flag_ref[2]
    for d in range(HEADS):
        for c in weight_copies(flag_ref[3], w_refs, d, Q_AT, 96, ws.at[d], sems.at[d]):
            c.start()
    xs = (x0_ref[...], x1_ref[...])
    ns = [norm(x.astype(F32), gain_ref[...]) for x in xs]
    cols = [[x[:, g * FW : (g + 1) * FW] for g in range(HEADS)] for x in xs]
    for d in range(HEADS):
        there = lax.rem(head + d, HEADS)
        wait_all(ws.at[d], sems.at[d])
        w = ws[d].reshape(FW, D)
        for i in range(2):
            q = mm_nt(ns[i], w).astype(BF)
            c = cols[i]
            e = jnp.where(
                there < 2, jnp.where(there == 0, c[0], c[1]), jnp.where(there == 2, c[2], c[3])
            )
            qe = jnp.concatenate([q, e], axis=1)
            if d == 2:
                (up_ref, down_ref)[i][SPAN:, :] = qe
            else:
                whole[d][pl.ds(i * BLK, BLK), :] = qe


def query(flags, x0, x1, gain, weights):
    return pl.pallas_call(
        query_body,
        out_shape=(
            jax.ShapeDtypeStruct((SPAN, 2 * FW), BF),
            jax.ShapeDtypeStruct((SPAN + BLK, 2 * FW), BF),
            jax.ShapeDtypeStruct((SPAN + BLK, 2 * FW), BF),
        ),
        in_specs=[SMEM, VMEM, VMEM, VMEM] + [ANY] * 16,
        out_specs=[VMEM] * 3,
        scratch_shapes=[
            pltpu.VMEM((HEADS, 2, 96, D), BF),
            pltpu.SemaphoreType.DMA((HEADS,)),
        ],
        compiler_params=params(12),
        cost_estimate=cost(4),
        name="fast_query",
    )(flags, x0, x1, gain, *weights)


def make_fast_body(blocks, first, last):
    def body(*refs):
        kv_refs = refs[:blocks]
        gu_ref, down_ref = refs[blocks : blocks + 2]
        sum_ref = None if first else refs[blocks + 2]
        g_ref = refs[-1]
        gate_up = [gu_ref[i].astype(BF) for i in range(2)]
        down = down_ref[...].astype(BF)
        sums = None
        for kv_ref in kv_refs:
            key = kv_ref[:, :FW]
            out_grad = kv_ref[:, FW:]
            gate = mm(key, gate_up[0])
            up = mm(key, gate_up[1])
            hidden_grad = mm(out_grad, down)
            s = jax.nn.sigmoid(gate)
            silu = gate * s
            hidden = (silu * up).astype(BF)
            gate_grad = (hidden_grad * up * s * (1.0 + gate * (1.0 - s))).astype(BF)
            up_grad = (hidden_grad * silu).astype(BF)
            parts = [mm_tn(key, gate_grad), mm_tn(key, up_grad), mm_tn(out_grad, hidden)]
            sums = parts if sums is None else [a + b for a, b in zip(sums, parts)]
        for i, total in enumerate(sums):
            if not first:
                total = total + sum_ref[i]
            if last:
                for t in range(LT):
                    g_ref[pl.ds((i * LT + t) * 24, 24)] = (
                        total[:, t * 128 : (t + 1) * 128].astype(BF).reshape(24, 8, 128)
                    )
            else:
                g_ref[i] = total
        if last:
            g_ref[pl.ds(216, 8)] = jnp.zeros((8, 8, 128), BF)

    return body


def fast(blocks, shared, sums, last):
    first = sums is None
    operands = (*blocks, *shared) + (() if first else (sums,))
    return pl.pallas_call(
        make_fast_body(len(blocks), first, last),
        out_shape=(
            jax.ShapeDtypeStruct((GT, 8, 128), BF)
            if last
            else jax.ShapeDtypeStruct((3, FW, FH), F32)
        ),
        in_specs=[VMEM] * len(operands),
        out_specs=VMEM,
        compiler_params=params(16),
        cost_estimate=cost(3),
        name="fast_grad",
    )(*operands)


def sum_body(x_ref, o_ref):
    total = x_ref[0].astype(F32)
    for i in range(1, SEQ):
        total = total + x_ref[i].astype(F32)
    total = total.astype(BF)
    for i in range(SEQ):
        o_ref[i] = total


def sum_pieces(x):
    return pl.pallas_call(
        sum_body,
        out_shape=jax.ShapeDtypeStruct(x.shape, BF),
        in_specs=[VMEM],
        out_specs=VMEM,
        compiler_params=params(4),
        cost_estimate=cost(1),
        name="sum_pieces",
    )(x)


def renorm(updated, initial, axis):
    target = jnp.sqrt(jnp.sum(initial * initial, axis=axis, keepdims=True))
    return updated * target * lax.rsqrt(jnp.sum(updated * updated, axis=axis, keepdims=True) + EPSILON)


def apply_body(head_ref, g_ref, gu_ref, down_ref, *refs):
    qe_refs, (o_ref, gs, ws) = refs[:5], refs[5:]
    for i in range(3):
        for t in range(LT):
            gs[i, :, pl.ds(t * 128, 128)] = (
                g_ref[pl.ds((i * LT + t) * 24, 24)].astype(F32).reshape(FW, 128)
            )
        init = down_ref[...] if i == 2 else gu_ref[i]
        ws[i] = renorm(init - gs[i], init, 0 if i == 2 else 1).astype(BF)
    row = lax.broadcasted_iota(jnp.int32, (FW, 2 * FW), 0)
    col = lax.broadcasted_iota(jnp.int32, (FW, 2 * FW), 1)
    columns = jnp.where(row + FW == col, 1.0, 0.0).astype(BF)
    own_ref, up_ref, down_side_ref, far0_ref, far1_ref = qe_refs
    for d in range(HEADS):
        if d == 2:
            qe = jnp.concatenate([far0_ref[...], far1_ref[...]], axis=0)
        else:
            qe = {0: own_ref, 1: up_ref, 3: down_side_ref}[d][:SPAN, :]
        q = qe[:, :FW]
        gate = mm(q, ws[0])
        hidden = (gate * jax.nn.sigmoid(gate) * mm(q, ws[1])).astype(BF)
        base = pl.multiple_of(lax.rem(head_ref[2] + HEADS - d, HEADS) * SPAN, SPAN)
        o_ref[:, pl.ds(base, SPAN)] = (mm_nt(columns, qe) + mm_nt(ws[2], hidden)).astype(BF)


def apply(flags, grads, gate_up, down, qes):
    return pl.pallas_call(
        apply_body,
        out_shape=jax.ShapeDtypeStruct((FW, HEADS * SPAN), BF),
        in_specs=[SMEM] + [VMEM] * 8,
        out_specs=VMEM,
        scratch_shapes=[pltpu.VMEM((3, FW, FH), F32), pltpu.VMEM((3, FW, FH), BF)],
        compiler_params=params(16),
        cost_estimate=cost(3),
        name="apply_fast",
    )(flags, grads, gate_up, down, *qes)


def exchange(x, axes):
    return lax.all_to_all(x, axes, split_axis=0, concat_axis=0, tiled=True)


def shifted(x, by):
    return lax.ppermute(x, "head", [(i, (i + by) % HEADS) for i in range(HEADS)])


def swapped(x):
    return lax.ppermute(x, "core", [(0, 1), (1, 0)])


def on_device(
    patches,
    slot_image,
    slot_dest,
    enc_gain,
    w_qkv,
    w_out,
    fast_gain,
    w_fast,
    w_rate,
    fast_gate_up,
    fast_down,
):
    head = lax.axis_index("head")
    core = lax.axis_index("core")
    seq = lax.axis_index(SEQ_AXES)
    at = jnp.stack([seq * HEADS + head, head, core]).astype(jnp.int32)

    ids = jnp.concatenate([slot_dest, slot_image]).astype(BF)
    tile = jnp.pad(ids[None, :], ((0, 7), (0, 96)))
    pieces, low, high = spread(
        at,
        patches.reshape(-1, 8, D),
        tile,
        jnp.transpose(w_qkv, (0, 2, 1)).reshape(3 * FW, D),
        w_out,
        jnp.transpose(w_fast, (0, 2, 1)).reshape(3 * FW, D),
        jnp.broadcast_to(w_rate.T, (16, D)),
    )
    before = (shifted(low, 1), shifted(high, 1))
    after = (shifted(low, -1), shifted(high, -1))
    picked, flags = pick(at, exchange(pieces, SEQ_AXES))
    picked, before, after = lax.optimization_barrier((picked, before, after))
    mine = exchange(picked, ALL_AXES)
    far = (shifted(before[0], 1), shifted(after[1], -1))
    weights = (low, high, *after, *far, *before)
    weights = [in_hbm(w) for w in weights + tuple(swapped(w) for w in weights)]

    fgain = fast_gain.reshape(1, D)
    own_0, *outs = encode_first(
        flags, mine.reshape(SEQ, 4, LT, 8, 128), enc_gain.reshape(1, D), fgain, weights
    )
    kv_0, carried = tuple(outs[:HEADS]), outs[HEADS:]
    got_0 = tuple(shifted(kv_0[d], d) for d in range(1, HEADS))
    own_1, *kv_1 = encode_second(flags, fgain, *carried, weights)
    kv_1 = tuple(kv_1)
    kv_1, got_0 = lax.optimization_barrier((kv_1, got_0))
    got_1 = tuple(shifted(kv_1[d], d) for d in range(1, HEADS))

    gate_up = fast_gate_up[0]
    down = fast_down[0].T
    sums = fast((kv_0[0], kv_1[0]), (gate_up, down), None, False)
    sums = fast(got_0, (gate_up, down), sums, False)
    qe = query(flags, own_0, own_1, fgain, weights)
    got_1, qe = lax.optimization_barrier((got_1, tuple(qe)))
    grads = fast(got_1, (gate_up, down), sums, True)

    own_qe, up_qe, down_qe = qe
    up_qe, down_qe = shifted(up_qe, 1), shifted(down_qe, -1)
    far_qe = (shifted(up_qe[SPAN:], 1), shifted(down_qe[SPAN:], -1))
    arrived = exchange(grads, SEQ_AXES)
    whole = exchange(sum_pieces(arrived.reshape(SEQ, GT // SEQ, 8, 128)), SEQ_AXES)
    return apply(
        flags,
        whole.reshape(GT, 8, 128),
        gate_up,
        down,
        (own_qe, up_qe, down_qe, *far_qe),
    ).T


def solution(mesh):
    fine = Mesh(mesh.devices.reshape(4, 4, 2, HEADS), ALL_AXES)
    in_specs = (
        P(SEQ_AXES, None),
        P(SEQ_AXES),
        P(SEQ_AXES),
        P(),
        P(None, None, "head"),
        P("head", None),
        P(),
        P(None, None, "head"),
        P(None, "head"),
        P("head", None, None, None),
        P("head", None, None),
    )
    return jax.shard_map(
        on_device, mesh=fine, in_specs=in_specs, out_specs=P(SEQ_AXES, "head"), check_vma=False
    )
```

```python
import jax
import jax.numpy as jnp
from jax import lax
from jax.experimental import pallas as pl
from jax.experimental.pallas import tpu as pltpu
from jax.sharding import Mesh, PartitionSpec as P

D = 768
HDIM = 64
BLK = 256
SPAN = 512
FW = 192
FH = 384
SEQ = 32
HEADS = 4
PAIRS = 8
LT = 3
GT = 224
WROWS = 688
KV_AT = 384
RATE_AT = 576
Q_AT = 592
CUT = 352
EPSILON = 1e-06
LOG2E = 1.4426950408889634
RATE_SCALE = 0.1
VTOKENS = 65536
BF = jnp.bfloat16
F32 = jnp.float32
SEQ_AXES = ("x", "z", "core")
ALL_AXES = ("x", "z", "core", "head")


def params(mib):
    return pltpu.CompilerParams(vmem_limit_bytes=mib << 20)


def cost(us):
    return pl.CostEstimate(flops=0, bytes_accessed=int(us * 3.6e6), transcendentals=0)


ANY = pl.BlockSpec(memory_space=pltpu.HBM)
SMEM = pl.BlockSpec(memory_space=pltpu.SMEM)
VMEM = pl.BlockSpec(memory_space=pltpu.VMEM)


def in_hbm(x):
    return pltpu.with_memory_space_constraint(x, pltpu.HBM)


def mm(a, b):
    return jnp.dot(a, b, preferred_element_type=F32)


def mm_nt(a, b):
    return lax.dot_general(a, b, (((1,), (1,)), ((), ())), preferred_element_type=F32)


def mm_tn(a, b):
    return lax.dot_general(a, b, (((0,), (0,)), ((), ())), preferred_element_type=F32)


def norm(rows, gain):
    factor = lax.rsqrt(jnp.mean(rows * rows, axis=-1, keepdims=True) + EPSILON)
    return (rows * factor * gain).astype(BF)


def spread_body(
    at_ref, dest_hbm, image_hbm, x_ref, rate_hbm, qkv_ref, out_ref, fast_ref,
    o_ref, low_ref, high_ref, buf, o_buf, w_ref, dest_ref, image_ref, rate_ref,
    sems, wsems, osem, psem, ssem,
):
    head = at_ref[1]
    core = at_ref[2]
    parity = lax.shift_right_logical(head, 1)
    half = head & 1
    small = [
        pltpu.make_async_copy(dest_hbm, dest_ref, ssem.at[0]),
        pltpu.make_async_copy(image_hbm, image_ref, ssem.at[1]),
        pltpu.make_async_copy(rate_hbm, rate_ref, ssem.at[2]),
    ]
    for c in small:
        c.start()
    copies = []
    for p in range(PAIRS):
        copies.append(
            pltpu.make_async_copy(
                x_ref.at[
                    pl.ds(p * 64 + parity * 32, SEQ), :, pl.ds(pl.multiple_of(half * FH, 128), FH)
                ],
                buf.at[p],
                sems.at[p],
            )
        )
        copies[p].start()

    def rows(ref, start, count):
        return ref.at[pl.ds(pl.multiple_of(start, 32), count)]

    moves = [
        (rows(qkv_ref, core * 288, 288), w_ref.at[pl.ds(0, 288)]),
        (rows(out_ref, core * 96, 96), w_ref.at[pl.ds(288, 96)]),
        (rows(fast_ref, FW + core * FW, FW), w_ref.at[pl.ds(KV_AT, FW)]),
        (rows(fast_ref, core * 96, 96), w_ref.at[pl.ds(Q_AT, 96)]),
    ]
    moves = [pltpu.make_async_copy(*m, wsems.at[i]) for i, m in enumerate(moves)]
    for m in moves:
        m.start()
    for c in small:
        c.wait()
    w_ref[pl.ds(RATE_AT, 16), :] = jnp.broadcast_to(rate_ref[...], (16, D))
    row = lax.broadcasted_iota(jnp.int32, (8, 128), 0)
    lane = jnp.where(row == 0, lax.broadcasted_iota(jnp.int32, (8, 128), 1), 128)
    tile = jnp.zeros((8, 128), F32)
    for i in range(16):
        tile = jnp.where(lane == i, dest_ref[i].astype(F32), tile)
        tile = jnp.where(lane == 16 + i, image_ref[i].astype(F32), tile)
    o_buf[PAIRS, :, 0] = jnp.broadcast_to(tile.astype(BF)[None], (SEQ, 8, 128))
    puts = [pltpu.make_async_copy(o_buf.at[PAIRS, :, 0], o_ref.at[:, PAIRS * LT], psem.at[PAIRS])]
    puts[0].start()
    for m in moves:
        m.wait()
    outs = [
        pltpu.make_async_copy(w_ref.at[pl.ds(0, CUT)], low_ref, osem.at[0]),
        pltpu.make_async_copy(w_ref.at[pl.ds(CUT, WROWS - CUT)], high_ref, osem.at[1]),
    ]
    for c in outs:
        c.start()
    for p in range(PAIRS):
        copies[p].wait()
        for t in range(LT):
            o_buf[p, :, t] = buf[p, :, :, t * 128 : (t + 1) * 128]
        puts.append(
            pltpu.make_async_copy(o_buf.at[p], o_ref.at[:, pl.ds(p * LT, LT)], psem.at[p])
        )
        puts[-1].start()
    for c in outs + puts:
        c.wait()


def spread(at, dest, image, x, rate, *weights):
    return pl.pallas_call(
        spread_body,
        out_shape=(
            pltpu.HBM((SEQ, PAIRS * LT + 1, 8, 128), BF),
            pltpu.HBM((CUT, D), BF),
            pltpu.HBM((WROWS - CUT, D), BF),
        ),
        in_specs=[SMEM] + [ANY] * 7,
        out_specs=[ANY] * 3,
        scratch_shapes=[
            pltpu.VMEM((PAIRS, SEQ, 8, FH), BF),
            pltpu.VMEM((PAIRS + 1, SEQ, LT, 8, 128), BF),
            pltpu.VMEM((WROWS, D), BF),
            pltpu.SMEM((16,), jnp.int32),
            pltpu.SMEM((16,), jnp.int32),
            pltpu.VMEM((1, D), BF),
            pltpu.SemaphoreType.DMA((PAIRS,)),
            pltpu.SemaphoreType.DMA((4,)),
            pltpu.SemaphoreType.DMA((2,)),
            pltpu.SemaphoreType.DMA((PAIRS + 1,)),
            pltpu.SemaphoreType.DMA((3,)),
        ],
        compiler_params=params(12),
        cost_estimate=cost(3),
        name="spread",
    )(at, *[in_hbm(a) for a in (dest, image, x, rate, *weights)])


def pick_body(at_ref, x_ref, o_ref, flag_ref, ids, table, source, sem):
    ids[...] = x_ref[:, PAIRS * LT, 0, :].astype(F32).astype(jnp.int32)
    copy = pltpu.make_async_copy(ids, table, sem)
    copy.start()
    copy.wait()

    def note(i, carry):
        for p in range(PAIRS):
            first = table[i, 2 * p]
            pair = jnp.minimum(lax.shift_right_arithmetic(first, 1), SEQ * HEADS - 1)
            source[jnp.where(first >= 0, pair, SEQ * HEADS)] = i * PAIRS + p
        return carry

    lax.fori_loop(0, SEQ, note, 0, unroll=2)

    def move(m, carry):
        q = source[m]
        at = (q & (PAIRS - 1)) * LT
        o_ref[m] = x_ref[lax.shift_right_logical(q, 3), pl.ds(at, LT)]
        return carry

    lax.fori_loop(0, SEQ * HEADS, move, 0, unroll=16)
    q = source[at_ref[0]]
    origin = lax.shift_right_logical(q, 3)
    slot = (q & (PAIRS - 1)) * 2
    flag_ref[0] = table[origin, slot] & 1
    flag_ref[1] = jnp.where(table[origin, 16 + slot] == table[origin, 17 + slot], 1, 0)
    flag_ref[2] = at_ref[1]
    flag_ref[3] = at_ref[2]


def pick(at, x):
    return pl.pallas_call(
        pick_body,
        out_shape=(
            jax.ShapeDtypeStruct((SEQ * HEADS, LT, 8, 128), BF),
            jax.ShapeDtypeStruct((4,), jnp.int32),
        ),
        in_specs=[SMEM, VMEM],
        out_specs=[VMEM, SMEM],
        scratch_shapes=[
            pltpu.VMEM((SEQ, 128), jnp.int32),
            pltpu.SMEM((SEQ, 128), jnp.int32),
            pltpu.SMEM((SEQ * HEADS + 8,), jnp.int32),
            pltpu.SemaphoreType.DMA(()),
        ],
        compiler_params=params(8),
        cost_estimate=cost(3),
        name="pick",
    )(at, x)


def weight_copies(core, w_refs, d, start, count, dst, sem):
    copies = []
    low = max(0, min(count, CUT - start))
    for side in range(2):
        to = dst.at[core if side == 0 else 1 - core]
        low_ref, high_ref = w_refs[side * 8 + d * 2 : side * 8 + d * 2 + 2]
        pieces = [(low_ref, start, 0, low), (high_ref, start + low - CUT, low, count - low)]
        for ref, at, put, n in pieces:
            if n:
                copies.append(
                    pltpu.make_async_copy(ref.at[pl.ds(at, n)], to.at[pl.ds(put, n)], sem)
                )
    return copies


def wait_all(dst, sem):
    pltpu.make_async_copy(dst, dst, sem).wait()


def attend(block, bias, q, k, v):
    lane = lax.broadcasted_iota(jnp.int32, (BLK, FW), 1)
    out = None
    for j in range(FW // HDIM):
        mine = (lane >= j * HDIM) & (lane < (j + 1) * HDIM)
        s = mm_nt(jnp.where(mine, q, jnp.zeros_like(q)), k)
        parts = [s[:, :BLK], s[:, BLK:]]
        parts[1 - block] = parts[1 - block] + bias
        top = jnp.max(jnp.maximum(parts[0], parts[1]), axis=-1, keepdims=True)
        p = jnp.concatenate([jnp.exp2(x - top).astype(BF) for x in parts], axis=1)
        o = mm(p, v)
        o = o[:, :FW] * (1.0 / o[:, FW : FW + 1])
        out = o if out is None else jnp.where(mine, o, out)
    return out.astype(BF)


def project(block, gain, fs, fsems, kv_refs):
    n = norm(block.astype(F32), gain)
    lane = lax.broadcasted_iota(jnp.int32, (BLK, 2 * FW), 1)
    for d in range(HEADS):
        wait_all(fs.at[d], fsems.at[d])
    z = mm_nt(n, jnp.concatenate([fs[d, 0, FW:] for d in range(HEADS)], axis=0))
    soft = jnp.maximum(z, 0.0) + jnp.log1p(jnp.exp(-jnp.abs(z)))
    rates = -(RATE_SCALE * VTOKENS**-0.5) * soft
    for d, kv_ref in enumerate(kv_refs):
        kv = mm_nt(n, fs[d, :, :FW].reshape(2 * FW, D)).astype(BF).astype(F32)
        kv_ref[...] = jnp.where(lane < FW, kv, kv * rates[:, d * 16 : d * 16 + 1]).astype(BF)


def encode_first_body(
    flag_ref, x_ref, gain_ref, fgain_ref, *refs
):
    w_refs = refs[:16]
    o_ref, kv0, kv1, kv2, kv3, q_ref, k_ref, v_ref, rest_ref = refs[16:25]
    xs, ns, ws, fs, sems, fsems = refs[25:]
    core = flag_ref[3]
    for d in range(HEADS):
        for c in weight_copies(core, w_refs, d, 0, FH, ws.at[d], sems.at[d]):
            c.start()
    for d in range(HEADS):
        for c in weight_copies(core, w_refs, d, KV_AT, FW + 16, fs.at[d], fsems.at[d]):
            c.start()
    flip = flag_ref[0]
    bias = jnp.where(flag_ref[1] != 0, 0.0, -1e30).astype(F32)
    for b in range(2):
        base = pl.multiple_of(jnp.bitwise_xor(flip, b) * BLK, BLK)
        for c in range(2):
            for t in range(LT):
                xs[pl.ds(base, BLK), pl.ds(c * FH + t * 128, 128)] = (
                    x_ref[:, 2 * b + c, t].astype(F32).reshape(BLK, 128)
                )
    gain = gain_ref[...]
    for r in range(8):
        ns[pl.ds(r * 64, 64), :] = norm(xs[pl.ds(r * 64, 64), :], gain)
    rest_ref[...] = xs[BLK:, :].astype(BF)
    n = ns[...]
    scale = HDIM**-0.5 * LOG2E
    out = xs[:BLK, :]
    for g in range(HEADS):
        wait_all(ws.at[g], sems.at[g])
        w = ws[g, :, : 3 * 96].reshape(3 * FW, D)
        q = (mm_nt(n, w[:FW]) * scale).astype(BF)
        k = mm_nt(n, w[FW : 2 * FW]).astype(BF)
        v = jnp.concatenate(
            [mm_nt(n, w[2 * FW :]).astype(BF), jnp.ones((SPAN, HDIM), BF)], axis=1
        )
        q_ref[g] = q[BLK:]
        k_ref[g] = k
        v_ref[g] = v
        att = attend(0, bias, q[:BLK], k, v)
        out = out + mm(att, ws[g, :, 3 * 96 :].reshape(FW, D))
    out = out.astype(BF)
    o_ref[...] = out
    project(out, fgain_ref[...], fs, fsems, (kv0, kv1, kv2, kv3))


def encode_first(flags, x, gain, fgain, weights):
    return pl.pallas_call(
        encode_first_body,
        out_shape=(
            jax.ShapeDtypeStruct((BLK, D), BF),
            *[jax.ShapeDtypeStruct((BLK, 2 * FW), BF)] * HEADS,
            jax.ShapeDtypeStruct((HEADS, BLK, FW), BF),
            jax.ShapeDtypeStruct((HEADS, SPAN, FW), BF),
            jax.ShapeDtypeStruct((HEADS, SPAN, FW + HDIM), BF),
            jax.ShapeDtypeStruct((BLK, D), BF),
        ),
        in_specs=[SMEM, VMEM, VMEM, VMEM] + [ANY] * 16,
        out_specs=[VMEM] * 9,
        scratch_shapes=[
            pltpu.VMEM((SPAN, D), F32),
            pltpu.VMEM((SPAN, D), BF),
            pltpu.VMEM((HEADS, 2, FH, D), BF),
            pltpu.VMEM((HEADS, 2, FW + 16, D), BF),
            pltpu.SemaphoreType.DMA((HEADS,)),
            pltpu.SemaphoreType.DMA((HEADS,)),
        ],
        compiler_params=params(24),
        cost_estimate=cost(9),
        name="encode_first",
    )(flags, x, gain, fgain, *weights)


def encode_second_body(
    flag_ref, fgain_ref, q_ref, k_ref, v_ref, rest_ref, *refs
):
    w_refs = refs[:16]
    o_ref, kv0, kv1, kv2, kv3, ws, fs, sem, fsems = refs[16:]
    core = flag_ref[3]
    for d in range(HEADS):
        for c in weight_copies(core, w_refs, d, 3 * 96, 96, ws.at[d], sem):
            c.start()
    for d in range(HEADS):
        for c in weight_copies(core, w_refs, d, KV_AT, FW + 16, fs.at[d], fsems.at[d]):
            c.start()
    bias = jnp.where(flag_ref[1] != 0, 0.0, -1e30).astype(F32)
    out = rest_ref[...].astype(F32)
    for g in range(HEADS):
        att = attend(1, bias, q_ref[g], k_ref[g], v_ref[g])
        if g == 0:
            wait_all(ws, sem)
        out = out + mm(att, ws[g].reshape(FW, D))
    out = out.astype(BF)
    o_ref[...] = out
    project(out, fgain_ref[...], fs, fsems, (kv0, kv1, kv2, kv3))


def encode_second(flags, fgain, q, k, v, rest, weights):
    return pl.pallas_call(
        encode_second_body,
        out_shape=(
            jax.ShapeDtypeStruct((BLK, D), BF),
            *[jax.ShapeDtypeStruct((BLK, 2 * FW), BF)] * HEADS,
        ),
        in_specs=[SMEM] + [VMEM] * 5 + [ANY] * 16,
        out_specs=[VMEM] * 5,
        scratch_shapes=[
            pltpu.VMEM((HEADS, 2, 96, D), BF),
            pltpu.VMEM((HEADS, 2, FW + 16, D), BF),
            pltpu.SemaphoreType.DMA(()),
            pltpu.SemaphoreType.DMA((HEADS,)),
        ],
        compiler_params=params(16),
        cost_estimate=cost(20),
        name="encode_second",
    )(flags, fgain, q, k, v, rest, *weights)


def query_body(flag_ref, x0_ref, x1_ref, gain_ref, *refs):
    w_refs = refs[:16]
    own_ref, up_ref, down_ref, ws, sems = refs[16:]
    whole = {0: own_ref, 1: up_ref, 3: down_ref}
    head = flag_ref[2]
    for d in range(HEADS):
        for c in weight_copies(flag_ref[3], w_refs, d, Q_AT, 96, ws.at[d], sems.at[d]):
            c.start()
    xs = (x0_ref[...], x1_ref[...])
    ns = [norm(x.astype(F32), gain_ref[...]) for x in xs]
    cols = [[x[:, g * FW : (g + 1) * FW] for g in range(HEADS)] for x in xs]
    for d in range(HEADS):
        there = ((head + d) & (HEADS - 1))
        wait_all(ws.at[d], sems.at[d])
        w = ws[d].reshape(FW, D)
        for i in range(2):
            q = mm_nt(ns[i], w).astype(BF)
            c = cols[i]
            e = jnp.where(
                there < 2, jnp.where(there == 0, c[0], c[1]), jnp.where(there == 2, c[2], c[3])
            )
            qe = jnp.concatenate([q, e], axis=1)
            if d == 2:
                (up_ref, down_ref)[i][SPAN:, :] = qe
            else:
                whole[d][pl.ds(i * BLK, BLK), :] = qe


def query(flags, x0, x1, gain, weights):
    return pl.pallas_call(
        query_body,
        out_shape=(
            jax.ShapeDtypeStruct((SPAN, 2 * FW), BF),
            jax.ShapeDtypeStruct((SPAN + BLK, 2 * FW), BF),
            jax.ShapeDtypeStruct((SPAN + BLK, 2 * FW), BF),
        ),
        in_specs=[SMEM, VMEM, VMEM, VMEM] + [ANY] * 16,
        out_specs=[VMEM] * 3,
        scratch_shapes=[
            pltpu.VMEM((HEADS, 2, 96, D), BF),
            pltpu.SemaphoreType.DMA((HEADS,)),
        ],
        compiler_params=params(12),
        cost_estimate=cost(4),
        name="fast_query",
    )(flags, x0, x1, gain, *weights)


def make_fast_body(blocks, first, last):
    def body(*refs):
        kv_refs = refs[:blocks]
        gu_ref, down_ref = refs[blocks : blocks + 2]
        sum_ref = None if first else refs[blocks + 2]
        g_ref = refs[-1]
        gate_up = [gu_ref[i].astype(BF) for i in range(2)]
        down = down_ref[...].astype(BF)
        sums = None
        for kv_ref in kv_refs:
            key = kv_ref[:, :FW]
            out_grad = kv_ref[:, FW:]
            gate = mm(key, gate_up[0])
            up = mm(key, gate_up[1])
            hidden_grad = mm(out_grad, down)
            s = jax.nn.sigmoid(gate)
            silu = gate * s
            hidden = (silu * up).astype(BF)
            gate_grad = (hidden_grad * up * s * (1.0 + gate * (1.0 - s))).astype(BF)
            up_grad = (hidden_grad * silu).astype(BF)
            parts = [mm_tn(key, gate_grad), mm_tn(key, up_grad), mm_tn(out_grad, hidden)]
            sums = parts if sums is None else [a + b for a, b in zip(sums, parts)]
        for i, total in enumerate(sums):
            if not first:
                total = total + sum_ref[i]
            if last:
                for t in range(LT):
                    g_ref[pl.ds((i * LT + t) * 24, 24)] = (
                        total[:, t * 128 : (t + 1) * 128].astype(BF).reshape(24, 8, 128)
                    )
            else:
                g_ref[i] = total
        if last:
            g_ref[pl.ds(216, 8)] = jnp.zeros((8, 8, 128), BF)

    return body


def fast(blocks, shared, sums, last):
    first = sums is None
    operands = (*blocks, *shared) + (() if first else (sums,))
    return pl.pallas_call(
        make_fast_body(len(blocks), first, last),
        out_shape=(
            jax.ShapeDtypeStruct((GT, 8, 128), BF)
            if last
            else jax.ShapeDtypeStruct((3, FW, FH), F32)
        ),
        in_specs=[VMEM] * len(operands),
        out_specs=VMEM,
        compiler_params=params(16),
        cost_estimate=cost(3),
        name="fast_grad",
    )(*operands)


def sum_body(x_ref, o_ref):
    total = x_ref[0].astype(F32)
    for i in range(1, SEQ):
        total = total + x_ref[i].astype(F32)
    total = total.astype(BF)
    for i in range(SEQ):
        o_ref[i] = total


def sum_pieces(x):
    return pl.pallas_call(
        sum_body,
        out_shape=jax.ShapeDtypeStruct(x.shape, BF),
        in_specs=[VMEM],
        out_specs=VMEM,
        compiler_params=params(4),
        cost_estimate=cost(1),
        name="sum_pieces",
    )(x)


def renorm(updated, initial, axis):
    target = jnp.sqrt(jnp.sum(initial * initial, axis=axis, keepdims=True))
    return updated * target * lax.rsqrt(jnp.sum(updated * updated, axis=axis, keepdims=True) + EPSILON)


def apply_body(head_ref, g_ref, gu_ref, down_ref, *refs):
    qe_refs, (o_ref, o_buf, gs, ws, sems) = refs[:5], refs[5:]
    for i in range(3):
        for t in range(LT):
            gs[i, :, pl.ds(t * 128, 128)] = (
                g_ref[pl.ds((i * LT + t) * 24, 24)].astype(F32).reshape(FW, 128)
            )
        init = down_ref[...] if i == 2 else gu_ref[i]
        ws[i] = renorm(init - gs[i], init, 0 if i == 2 else 1).astype(BF)
    row = lax.broadcasted_iota(jnp.int32, (FW, 2 * FW), 0)
    col = lax.broadcasted_iota(jnp.int32, (FW, 2 * FW), 1)
    columns = jnp.where(row + FW == col, 1.0, 0.0).astype(BF)
    own_ref, up_ref, down_side_ref, far0_ref, far1_ref = qe_refs
    puts = []
    for d in (0, 1, 3, 2):
        if d == 2:
            qe = jnp.concatenate([far0_ref[...], far1_ref[...]], axis=0)
        else:
            qe = {0: own_ref, 1: up_ref, 3: down_side_ref}[d][:SPAN, :]
        q = qe[:, :FW]
        gate = mm(q, ws[0])
        hidden = (gate * jax.nn.sigmoid(gate) * mm(q, ws[1])).astype(BF)
        base = pl.multiple_of(((head_ref[2] + HEADS - d) & (HEADS - 1)) * SPAN, SPAN)
        o_buf[d] = (mm_nt(columns, qe) + mm_nt(ws[2], hidden)).astype(BF)
        puts.append(
            pltpu.make_async_copy(o_buf.at[d], o_ref.at[:, pl.ds(base, SPAN)], sems.at[d])
        )
        puts[-1].start()
    for c in puts:
        c.wait()


def apply(flags, grads, gate_up, down, qes):
    return pl.pallas_call(
        apply_body,
        out_shape=pltpu.HBM((FW, HEADS * SPAN), BF),
        in_specs=[SMEM] + [VMEM] * 8,
        out_specs=ANY,
        scratch_shapes=[
            pltpu.VMEM((HEADS, FW, SPAN), BF),
            pltpu.VMEM((3, FW, FH), F32),
            pltpu.VMEM((3, FW, FH), BF),
            pltpu.SemaphoreType.DMA((HEADS,)),
        ],
        compiler_params=params(16),
        cost_estimate=cost(3),
        name="apply_fast",
    )(flags, grads, gate_up, down, *qes)


def exchange(x, axes):
    return lax.all_to_all(x, axes, split_axis=0, concat_axis=0, tiled=True)


def shifted(x, by):
    return lax.ppermute(x, "head", [(i, (i + by) % HEADS) for i in range(HEADS)])


def swapped(x):
    return lax.ppermute(x, "core", [(0, 1), (1, 0)])


def on_device(
    patches,
    slot_image,
    slot_dest,
    enc_gain,
    w_qkv,
    w_out,
    fast_gain,
    w_fast,
    w_rate,
    fast_gate_up,
    fast_down,
):
    head = lax.axis_index("head")
    core = lax.axis_index("core")
    seq = lax.axis_index(SEQ_AXES)
    at = jnp.stack([seq * HEADS + head, head, core]).astype(jnp.int32)

    pieces, low, high = spread(
        at,
        slot_dest,
        slot_image,
        patches.reshape(-1, 8, D),
        w_rate.T,
        jnp.transpose(w_qkv, (0, 2, 1)).reshape(3 * FW, D),
        w_out,
        jnp.transpose(w_fast, (0, 2, 1)).reshape(3 * FW, D),
    )
    before = (shifted(low, 1), shifted(high, 1))
    after = (shifted(low, -1), shifted(high, -1))
    picked, flags = pick(at, exchange(pieces, SEQ_AXES))
    picked, before, after = lax.optimization_barrier((picked, before, after))
    mine = exchange(picked, ALL_AXES)
    far = (shifted(before[0], 1), shifted(after[1], -1))
    weights = (low, high, *after, *far, *before)
    weights = [in_hbm(w) for w in weights + tuple(swapped(w) for w in weights)]

    fgain = fast_gain.reshape(1, D)
    own_0, *outs = encode_first(
        flags, mine.reshape(SEQ, 4, LT, 8, 128), enc_gain.reshape(1, D), fgain, weights
    )
    kv_0, carried = tuple(outs[:HEADS]), outs[HEADS:]
    got_0 = tuple(shifted(kv_0[d], d) for d in range(1, HEADS))
    own_1, *kv_1 = encode_second(flags, fgain, *carried, weights)
    kv_1 = tuple(kv_1)
    kv_1, got_0 = lax.optimization_barrier((kv_1, got_0))
    got_1 = tuple(shifted(kv_1[d], d) for d in range(1, HEADS))

    gate_up = fast_gate_up[0]
    down = fast_down[0].T
    sums = fast((kv_0[0], kv_1[0]), (gate_up, down), None, False)
    sums = fast(got_0, (gate_up, down), sums, False)
    qe = query(flags, own_0, own_1, fgain, weights)
    got_1, qe = lax.optimization_barrier((got_1, tuple(qe)))
    grads = fast(got_1, (gate_up, down), sums, True)

    own_qe, up_qe, down_qe = qe
    up_qe, down_qe = shifted(up_qe, 1), shifted(down_qe, -1)
    far_qe = (shifted(up_qe[SPAN:], 1), shifted(down_qe[SPAN:], -1))
    arrived = exchange(grads, SEQ_AXES)
    whole = exchange(sum_pieces(arrived.reshape(SEQ, GT // SEQ, 8, 128)), SEQ_AXES)
    return apply(
        flags,
        whole.reshape(GT, 8, 128),
        gate_up,
        down,
        (own_qe, up_qe, down_qe, *far_qe),
    ).T


def solution(mesh):
    fine = Mesh(mesh.devices.reshape(4, 4, 2, HEADS), ALL_AXES)
    in_specs = (
        P(SEQ_AXES, None),
        P(SEQ_AXES),
        P(SEQ_AXES),
        P(),
        P(None, None, "head"),
        P("head", None),
        P(),
        P(None, None, "head"),
        P(None, "head"),
        P("head", None, None, None),
        P("head", None, None),
    )
    return jax.shard_map(
        on_device, mesh=fine, in_specs=in_specs, out_specs=P(SEQ_AXES, "head"), check_vma=False
    )
```

```python
import jax
import jax.numpy as jnp
from jax import lax
from jax.experimental import pallas as pl
from jax.experimental.pallas import tpu as pltpu
from jax.sharding import Mesh, PartitionSpec as P

D = 768
HDIM = 64
BLK = 256
SPAN = 512
FW = 192
FH = 384
SEQ = 32
HEADS = 4
PAIRS = 8
LT = 3
GT = 224
WROWS = 688
KV_AT = 384
RATE_AT = 576
Q_AT = 592
CUT = 352
EPSILON = 1e-06
LOG2E = 1.4426950408889634
RATE_SCALE = 0.1
VTOKENS = 65536
BF = jnp.bfloat16
F32 = jnp.float32
SEQ_AXES = ("x", "z", "core")
ALL_AXES = ("x", "z", "core", "head")


def params(mib):
    return pltpu.CompilerParams(vmem_limit_bytes=mib << 20)


def cost(us):
    return pl.CostEstimate(flops=0, bytes_accessed=int(us * 3.6e6), transcendentals=0)


ANY = pl.BlockSpec(memory_space=pltpu.HBM)
SMEM = pl.BlockSpec(memory_space=pltpu.SMEM)
VMEM = pl.BlockSpec(memory_space=pltpu.VMEM)


def in_hbm(x):
    return pltpu.with_memory_space_constraint(x, pltpu.HBM)


def mm(a, b):
    return jnp.dot(a, b, preferred_element_type=F32)


def mm_nt(a, b):
    return lax.dot_general(a, b, (((1,), (1,)), ((), ())), preferred_element_type=F32)


def mm_tn(a, b):
    return lax.dot_general(a, b, (((0,), (0,)), ((), ())), preferred_element_type=F32)


def norm(rows, gain):
    factor = lax.rsqrt(jnp.mean(rows * rows, axis=-1, keepdims=True) + EPSILON)
    return (rows * factor * gain).astype(BF)


def spread_body(
    at_ref, dest_hbm, image_hbm, x_ref, rate_hbm, qkv_ref, out_ref, fast_ref,
    o_ref, low_ref, high_ref, buf, o_buf, w_ref, dest_ref, image_ref, rate_ref,
    sems, wsems, osem, psem, ssem,
):
    head = at_ref[1]
    core = at_ref[2]
    parity = lax.shift_right_logical(head, 1)
    half = head & 1
    small = [
        pltpu.make_async_copy(dest_hbm, dest_ref, ssem.at[0]),
        pltpu.make_async_copy(image_hbm, image_ref, ssem.at[1]),
        pltpu.make_async_copy(rate_hbm, rate_ref, ssem.at[2]),
    ]
    for c in small:
        c.start()
    copies = []
    for p in range(PAIRS):
        copies.append(
            pltpu.make_async_copy(
                x_ref.at[
                    pl.ds(p * 64 + parity * 32, SEQ), :, pl.ds(pl.multiple_of(half * FH, 128), FH)
                ],
                buf.at[p],
                sems.at[p],
            )
        )
        copies[p].start()

    def rows(ref, start, count):
        return ref.at[pl.ds(pl.multiple_of(start, 32), count)]

    moves = [
        (rows(qkv_ref, core * 288, 288), w_ref.at[pl.ds(0, 288)]),
        (rows(out_ref, core * 96, 96), w_ref.at[pl.ds(288, 96)]),
        (rows(fast_ref, FW + core * FW, FW), w_ref.at[pl.ds(KV_AT, FW)]),
        (rows(fast_ref, core * 96, 96), w_ref.at[pl.ds(Q_AT, 96)]),
    ]
    moves = [pltpu.make_async_copy(*m, wsems.at[i]) for i, m in enumerate(moves)]
    for m in moves:
        m.start()
    for c in small:
        c.wait()
    w_ref[pl.ds(RATE_AT, 16), :] = jnp.broadcast_to(rate_ref[...], (16, D))
    row = lax.broadcasted_iota(jnp.int32, (8, 128), 0)
    lane = jnp.where(row == 0, lax.broadcasted_iota(jnp.int32, (8, 128), 1), 128)
    tile = jnp.zeros((8, 128), F32)
    for i in range(16):
        tile = jnp.where(lane == i, dest_ref[i].astype(F32), tile)
        tile = jnp.where(lane == 16 + i, image_ref[i].astype(F32), tile)
    o_buf[PAIRS, :, 0] = jnp.broadcast_to(tile.astype(BF)[None], (SEQ, 8, 128))
    puts = [pltpu.make_async_copy(o_buf.at[PAIRS, :, 0], o_ref.at[:, PAIRS * LT], psem.at[PAIRS])]
    puts[0].start()
    for m in moves:
        m.wait()
    outs = [
        pltpu.make_async_copy(w_ref.at[pl.ds(0, CUT)], low_ref, osem.at[0]),
        pltpu.make_async_copy(w_ref.at[pl.ds(CUT, WROWS - CUT)], high_ref, osem.at[1]),
    ]
    for c in outs:
        c.start()
    for p in range(PAIRS):
        copies[p].wait()
        for t in range(LT):
            o_buf[p, :, t] = buf[p, :, :, t * 128 : (t + 1) * 128]
        puts.append(
            pltpu.make_async_copy(o_buf.at[p], o_ref.at[:, pl.ds(p * LT, LT)], psem.at[p])
        )
        puts[-1].start()
    for c in outs + puts:
        c.wait()


def spread(at, dest, image, x, rate, *weights):
    return pl.pallas_call(
        spread_body,
        out_shape=(
            pltpu.HBM((SEQ, PAIRS * LT + 1, 8, 128), BF),
            pltpu.HBM((CUT, D), BF),
            pltpu.HBM((WROWS - CUT, D), BF),
        ),
        in_specs=[SMEM] + [ANY] * 7,
        out_specs=[ANY] * 3,
        scratch_shapes=[
            pltpu.VMEM((PAIRS, SEQ, 8, FH), BF),
            pltpu.VMEM((PAIRS + 1, SEQ, LT, 8, 128), BF),
            pltpu.VMEM((WROWS, D), BF),
            pltpu.SMEM((16,), jnp.int32),
            pltpu.SMEM((16,), jnp.int32),
            pltpu.VMEM((1, D), BF),
            pltpu.SemaphoreType.DMA((PAIRS,)),
            pltpu.SemaphoreType.DMA((4,)),
            pltpu.SemaphoreType.DMA((2,)),
            pltpu.SemaphoreType.DMA((PAIRS + 1,)),
            pltpu.SemaphoreType.DMA((3,)),
        ],
        compiler_params=params(12),
        cost_estimate=cost(3),
        name="spread",
    )(at, *[in_hbm(a) for a in (dest, image, x, rate, *weights)])


def pick_body(at_ref, x_ref, o_ref, flag_ref, ids, table, source, sem):
    ids[...] = x_ref[:, PAIRS * LT, 0, :].astype(F32).astype(jnp.int32)
    copy = pltpu.make_async_copy(ids, table, sem)
    copy.start()
    copy.wait()

    def note(i, carry):
        for p in range(PAIRS):
            first = table[i, 2 * p]
            pair = jnp.minimum(lax.shift_right_arithmetic(first, 1), SEQ * HEADS - 1)
            source[jnp.where(first >= 0, pair, SEQ * HEADS)] = i * PAIRS + p
        return carry

    lax.fori_loop(0, SEQ, note, 0, unroll=2)

    def move(m, carry):
        q = source[m]
        at = (q & (PAIRS - 1)) * LT
        o_ref[m] = x_ref[lax.shift_right_logical(q, 3), pl.ds(at, LT)]
        return carry

    lax.fori_loop(0, SEQ * HEADS, move, 0, unroll=16)
    q = source[at_ref[0]]
    origin = lax.shift_right_logical(q, 3)
    slot = (q & (PAIRS - 1)) * 2
    flag_ref[0] = table[origin, slot] & 1
    flag_ref[1] = jnp.where(table[origin, 16 + slot] == table[origin, 17 + slot], 1, 0)
    flag_ref[2] = at_ref[1]
    flag_ref[3] = at_ref[2]


def pick(at, x):
    return pl.pallas_call(
        pick_body,
        out_shape=(
            jax.ShapeDtypeStruct((SEQ * HEADS, LT, 8, 128), BF),
            jax.ShapeDtypeStruct((4,), jnp.int32),
        ),
        in_specs=[SMEM, VMEM],
        out_specs=[VMEM, SMEM],
        scratch_shapes=[
            pltpu.VMEM((SEQ, 128), jnp.int32),
            pltpu.SMEM((SEQ, 128), jnp.int32),
            pltpu.SMEM((SEQ * HEADS + 8,), jnp.int32),
            pltpu.SemaphoreType.DMA(()),
        ],
        compiler_params=params(8),
        cost_estimate=cost(3),
        name="pick",
    )(at, x)


def weight_copies(core, w_refs, d, start, count, dst, sem):
    copies = []
    low = max(0, min(count, CUT - start))
    for side in range(2):
        to = dst.at[core if side == 0 else 1 - core]
        low_ref, high_ref = w_refs[side * 8 + d * 2 : side * 8 + d * 2 + 2]
        pieces = [(low_ref, start, 0, low), (high_ref, start + low - CUT, low, count - low)]
        for ref, at, put, n in pieces:
            if n:
                copies.append(
                    pltpu.make_async_copy(ref.at[pl.ds(at, n)], to.at[pl.ds(put, n)], sem)
                )
    return copies


def wait_all(dst, sem):
    pltpu.make_async_copy(dst, dst, sem).wait()


def attend(block, bias, q, k, v):
    lane = lax.broadcasted_iota(jnp.int32, (BLK, FW), 1)
    out = None
    for j in range(FW // HDIM):
        mine = (lane >= j * HDIM) & (lane < (j + 1) * HDIM)
        s = mm_nt(jnp.where(mine, q, jnp.zeros_like(q)), k)
        parts = [s[:, :BLK], s[:, BLK:]]
        parts[1 - block] = parts[1 - block] + bias
        top = jnp.max(jnp.maximum(parts[0], parts[1]), axis=-1, keepdims=True)
        p = jnp.concatenate([jnp.exp2(x - top).astype(BF) for x in parts], axis=1)
        o = mm(p, v)
        o = o[:, :FW] * (1.0 / o[:, FW : FW + 1])
        out = o if out is None else jnp.where(mine, o, out)
    return out.astype(BF)


def project(block, gain, fs, fsems, kv_refs):
    n = norm(block.astype(F32), gain)
    lane = lax.broadcasted_iota(jnp.int32, (BLK, 2 * FW), 1)
    for d in range(HEADS):
        wait_all(fs.at[d], fsems.at[d])
    z = mm_nt(n, jnp.concatenate([fs[d, 0, FW:] for d in range(HEADS)], axis=0))
    soft = jnp.maximum(z, 0.0) + jnp.log1p(jnp.exp(-jnp.abs(z)))
    rates = -(RATE_SCALE * VTOKENS**-0.5) * soft
    for d, kv_ref in enumerate(kv_refs):
        kv = mm_nt(n, fs[d, :, :FW].reshape(2 * FW, D)).astype(BF).astype(F32)
        kv_ref[...] = jnp.where(lane < FW, kv, kv * rates[:, d * 16 : d * 16 + 1]).astype(BF)


def encode_first_body(
    flag_ref, x_ref, gain_ref, fgain_ref, *refs
):
    w_refs = refs[:16]
    o_ref, kv0, kv1, kv2, kv3, q_ref, k_ref, v_ref, rest_ref = refs[16:25]
    xs, ns, ws, fs, sems, fsems = refs[25:]
    core = flag_ref[3]
    for d in range(HEADS):
        for c in weight_copies(core, w_refs, d, 0, FH, ws.at[d], sems.at[d]):
            c.start()
    for d in range(HEADS):
        for c in weight_copies(core, w_refs, d, KV_AT, FW + 16, fs.at[d], fsems.at[d]):
            c.start()
    flip = flag_ref[0]
    bias = jnp.where(flag_ref[1] != 0, 0.0, -1e30).astype(F32)
    for b in range(2):
        base = pl.multiple_of(jnp.bitwise_xor(flip, b) * BLK, BLK)
        for c in range(2):
            for t in range(LT):
                xs[pl.ds(base, BLK), pl.ds(c * FH + t * 128, 128)] = (
                    x_ref[:, 2 * b + c, t].astype(F32).reshape(BLK, 128)
                )
    gain = gain_ref[...]
    for r in range(8):
        ns[pl.ds(r * 64, 64), :] = norm(xs[pl.ds(r * 64, 64), :], gain)
    rest_ref[...] = xs[BLK:, :].astype(BF)
    n = ns[...]
    scale = HDIM**-0.5 * LOG2E
    out = xs[:BLK, :]
    for g in range(HEADS):
        wait_all(ws.at[g], sems.at[g])
        w = ws[g, :, : 3 * 96].reshape(3 * FW, D)
        q = (mm_nt(n, w[:FW]) * scale).astype(BF)
        k = mm_nt(n, w[FW : 2 * FW]).astype(BF)
        v = jnp.concatenate(
            [mm_nt(n, w[2 * FW :]).astype(BF), jnp.ones((SPAN, HDIM), BF)], axis=1
        )
        q_ref[g] = q[BLK:]
        k_ref[g] = k
        v_ref[g] = v
        att = attend(0, bias, q[:BLK], k, v)
        out = out + mm(att, ws[g, :, 3 * 96 :].reshape(FW, D))
    out = out.astype(BF)
    o_ref[...] = out
    project(out, fgain_ref[...], fs, fsems, (kv0, kv1, kv2, kv3))


def encode_first(flags, x, gain, fgain, weights):
    return pl.pallas_call(
        encode_first_body,
        out_shape=(
            jax.ShapeDtypeStruct((BLK, D), BF),
            *[jax.ShapeDtypeStruct((BLK, 2 * FW), BF)] * HEADS,
            jax.ShapeDtypeStruct((HEADS, BLK, FW), BF),
            jax.ShapeDtypeStruct((HEADS, SPAN, FW), BF),
            jax.ShapeDtypeStruct((HEADS, SPAN, FW + HDIM), BF),
            jax.ShapeDtypeStruct((BLK, D), BF),
        ),
        in_specs=[SMEM, VMEM, VMEM, VMEM] + [ANY] * 16,
        out_specs=[VMEM] * 9,
        scratch_shapes=[
            pltpu.VMEM((SPAN, D), F32),
            pltpu.VMEM((SPAN, D), BF),
            pltpu.VMEM((HEADS, 2, FH, D), BF),
            pltpu.VMEM((HEADS, 2, FW + 16, D), BF),
            pltpu.SemaphoreType.DMA((HEADS,)),
            pltpu.SemaphoreType.DMA((HEADS,)),
        ],
        compiler_params=params(24),
        cost_estimate=cost(9),
        name="encode_first",
    )(flags, x, gain, fgain, *weights)


def encode_second_body(
    flag_ref, fgain_ref, q_ref, k_ref, v_ref, rest_ref, *refs
):
    w_refs = refs[:16]
    o_ref, kv0, kv1, kv2, kv3, ws, fs, sem, fsems = refs[16:]
    core = flag_ref[3]
    for d in range(HEADS):
        for c in weight_copies(core, w_refs, d, 3 * 96, 96, ws.at[d], sem):
            c.start()
    for d in range(HEADS):
        for c in weight_copies(core, w_refs, d, KV_AT, FW + 16, fs.at[d], fsems.at[d]):
            c.start()
    bias = jnp.where(flag_ref[1] != 0, 0.0, -1e30).astype(F32)
    out = rest_ref[...].astype(F32)
    for g in range(HEADS):
        att = attend(1, bias, q_ref[g], k_ref[g], v_ref[g])
        if g == 0:
            wait_all(ws, sem)
        out = out + mm(att, ws[g].reshape(FW, D))
    out = out.astype(BF)
    o_ref[...] = out
    project(out, fgain_ref[...], fs, fsems, (kv0, kv1, kv2, kv3))


def encode_second(flags, fgain, q, k, v, rest, weights):
    return pl.pallas_call(
        encode_second_body,
        out_shape=(
            jax.ShapeDtypeStruct((BLK, D), BF),
            *[jax.ShapeDtypeStruct((BLK, 2 * FW), BF)] * HEADS,
        ),
        in_specs=[SMEM] + [VMEM] * 5 + [ANY] * 16,
        out_specs=[VMEM] * 5,
        scratch_shapes=[
            pltpu.VMEM((HEADS, 2, 96, D), BF),
            pltpu.VMEM((HEADS, 2, FW + 16, D), BF),
            pltpu.SemaphoreType.DMA(()),
            pltpu.SemaphoreType.DMA((HEADS,)),
        ],
        compiler_params=params(16),
        cost_estimate=cost(20),
        name="encode_second",
    )(flags, fgain, q, k, v, rest, *weights)


def query_body(flag_ref, x0_ref, x1_ref, gain_ref, *refs):
    w_refs = refs[:16]
    own_ref, up_ref, down_ref, ws, sems = refs[16:]
    whole = {0: own_ref, 1: up_ref, 3: down_ref}
    head = flag_ref[2]
    for d in range(HEADS):
        for c in weight_copies(flag_ref[3], w_refs, d, Q_AT, 96, ws.at[d], sems.at[d]):
            c.start()
    xs = (x0_ref[...], x1_ref[...])
    ns = [norm(x.astype(F32), gain_ref[...]) for x in xs]
    cols = [[x[:, g * FW : (g + 1) * FW] for g in range(HEADS)] for x in xs]
    for d in range(HEADS):
        there = ((head + d) & (HEADS - 1))
        wait_all(ws.at[d], sems.at[d])
        w = ws[d].reshape(FW, D)
        for i in range(2):
            q = mm_nt(ns[i], w).astype(BF)
            c = cols[i]
            e = jnp.where(
                there < 2, jnp.where(there == 0, c[0], c[1]), jnp.where(there == 2, c[2], c[3])
            )
            qe = jnp.concatenate([q, e], axis=1)
            if d == 2:
                (up_ref, down_ref)[i][SPAN:, :] = qe
            else:
                whole[d][pl.ds(i * BLK, BLK), :] = qe


def query(flags, x0, x1, gain, weights):
    return pl.pallas_call(
        query_body,
        out_shape=(
            jax.ShapeDtypeStruct((SPAN, 2 * FW), BF),
            jax.ShapeDtypeStruct((SPAN + BLK, 2 * FW), BF),
            jax.ShapeDtypeStruct((SPAN + BLK, 2 * FW), BF),
        ),
        in_specs=[SMEM, VMEM, VMEM, VMEM] + [ANY] * 16,
        out_specs=[VMEM] * 3,
        scratch_shapes=[
            pltpu.VMEM((HEADS, 2, 96, D), BF),
            pltpu.SemaphoreType.DMA((HEADS,)),
        ],
        compiler_params=params(12),
        cost_estimate=cost(4),
        name="fast_query",
    )(flags, x0, x1, gain, *weights)


def make_fast_body(blocks, first, last):
    def body(*refs):
        kv_refs = refs[:blocks]
        gu_ref, down_ref = refs[blocks : blocks + 2]
        sum_ref = None if first else refs[blocks + 2]
        g_ref = refs[-1]
        gate_up = [gu_ref[i].astype(BF) for i in range(2)]
        down = down_ref[...].astype(BF)
        sums = None
        for kv_ref in kv_refs:
            key = kv_ref[:, :FW]
            out_grad = kv_ref[:, FW:]
            gate = mm(key, gate_up[0])
            up = mm(key, gate_up[1])
            hidden_grad = mm(out_grad, down)
            s = jax.nn.sigmoid(gate)
            silu = gate * s
            hidden = (silu * up).astype(BF)
            gate_grad = (hidden_grad * up * s * (1.0 + gate * (1.0 - s))).astype(BF)
            up_grad = (hidden_grad * silu).astype(BF)
            parts = [mm_tn(key, gate_grad), mm_tn(key, up_grad), mm_tn(out_grad, hidden)]
            sums = parts if sums is None else [a + b for a, b in zip(sums, parts)]
        for i, total in enumerate(sums):
            if not first:
                total = total + sum_ref[i]
            if last:
                for t in range(LT):
                    g_ref[pl.ds((i * LT + t) * 24, 24)] = (
                        total[:, t * 128 : (t + 1) * 128].astype(BF).reshape(24, 8, 128)
                    )
            else:
                g_ref[i] = total
        if last:
            g_ref[pl.ds(216, 8)] = jnp.zeros((8, 8, 128), BF)

    return body


def fast(blocks, shared, sums, last):
    first = sums is None
    operands = (*blocks, *shared) + (() if first else (sums,))
    return pl.pallas_call(
        make_fast_body(len(blocks), first, last),
        out_shape=(
            jax.ShapeDtypeStruct((GT, 8, 128), BF)
            if last
            else jax.ShapeDtypeStruct((3, FW, FH), F32)
        ),
        in_specs=[VMEM] * len(operands),
        out_specs=VMEM,
        compiler_params=params(16),
        cost_estimate=cost(3),
        name="fast_grad",
    )(*operands)


def sum_body(x_ref, o_ref):
    total = x_ref[0].astype(F32)
    for i in range(1, SEQ):
        total = total + x_ref[i].astype(F32)
    total = total.astype(BF)
    for i in range(SEQ):
        o_ref[i] = total


def sum_pieces(x):
    return pl.pallas_call(
        sum_body,
        out_shape=jax.ShapeDtypeStruct(x.shape, BF),
        in_specs=[VMEM],
        out_specs=VMEM,
        compiler_params=params(4),
        cost_estimate=cost(1),
        name="sum_pieces",
    )(x)


def renorm(updated, initial, axis):
    target = jnp.sqrt(jnp.sum(initial * initial, axis=axis, keepdims=True))
    return updated * target * lax.rsqrt(jnp.sum(updated * updated, axis=axis, keepdims=True) + EPSILON)


def apply_body(head_ref, g_ref, gu_ref, down_ref, *refs):
    qe_refs, (o_ref, o_buf, gs, ws, sems) = refs[:5], refs[5:]
    for i in range(3):
        for t in range(LT):
            gs[i, :, pl.ds(t * 128, 128)] = (
                g_ref[pl.ds((i * LT + t) * 24, 24)].astype(F32).reshape(FW, 128)
            )
        init = down_ref[...] if i == 2 else gu_ref[i]
        ws[i] = renorm(init - gs[i], init, 0 if i == 2 else 1).astype(BF)
    row = lax.broadcasted_iota(jnp.int32, (FW, 2 * FW), 0)
    col = lax.broadcasted_iota(jnp.int32, (FW, 2 * FW), 1)
    columns = jnp.where(row + FW == col, 1.0, 0.0).astype(BF)
    own_ref, up_ref, down_side_ref, far0_ref, far1_ref = qe_refs
    puts = []
    for d in (0, 1, 3, 2):
        if d == 2:
            qe = jnp.concatenate([far0_ref[...], far1_ref[...]], axis=0)
        else:
            qe = {0: own_ref, 1: up_ref, 3: down_side_ref}[d][:SPAN, :]
        q = qe[:, :FW]
        gate = mm(q, ws[0])
        hidden = (gate * jax.nn.sigmoid(gate) * mm(q, ws[1])).astype(BF)
        base = pl.multiple_of(((head_ref[2] + HEADS - d) & (HEADS - 1)) * SPAN, SPAN)
        o_buf[d] = (mm_nt(columns, qe) + mm_nt(ws[2], hidden)).astype(BF)
        puts.append(
            pltpu.make_async_copy(o_buf.at[d], o_ref.at[:, pl.ds(base, SPAN)], sems.at[d])
        )
        puts[-1].start()
    for c in puts:
        c.wait()


def apply(flags, grads, gate_up, down, qes):
    return pl.pallas_call(
        apply_body,
        out_shape=pltpu.HBM((FW, HEADS * SPAN), BF),
        in_specs=[SMEM] + [VMEM] * 8,
        out_specs=ANY,
        scratch_shapes=[
            pltpu.VMEM((HEADS, FW, SPAN), BF),
            pltpu.VMEM((3, FW, FH), F32),
            pltpu.VMEM((3, FW, FH), BF),
            pltpu.SemaphoreType.DMA((HEADS,)),
        ],
        compiler_params=params(16),
        cost_estimate=cost(3),
        name="apply_fast",
    )(flags, grads, gate_up, down, *qes)


def exchange(x, axes):
    return lax.all_to_all(x, axes, split_axis=0, concat_axis=0, tiled=True)


def shifted(x, by):
    return lax.ppermute(x, "head", [(i, (i + by) % HEADS) for i in range(HEADS)])


def swapped(x):
    return lax.ppermute(x, "core", [(0, 1), (1, 0)])


def on_device(
    patches,
    slot_image,
    slot_dest,
    enc_gain,
    w_qkv,
    w_out,
    fast_gain,
    w_fast,
    w_rate,
    fast_gate_up,
    fast_down,
):
    head = lax.axis_index("head")
    core = lax.axis_index("core")
    seq = lax.axis_index(SEQ_AXES)
    at = jnp.stack([seq * HEADS + head, head, core]).astype(jnp.int32)

    pieces, low, high = spread(
        at,
        slot_dest,
        slot_image,
        patches.reshape(-1, 8, D),
        w_rate.T,
        jnp.transpose(w_qkv, (0, 2, 1)).reshape(3 * FW, D),
        w_out,
        jnp.transpose(w_fast, (0, 2, 1)).reshape(3 * FW, D),
    )
    before = (shifted(low, 1), shifted(high, 1))
    after = (shifted(low, -1), shifted(high, -1))
    picked, flags = pick(at, exchange(pieces, SEQ_AXES))
    mine = exchange(picked, ALL_AXES)
    far = (shifted(before[0], 1), shifted(after[1], -1))
    weights = (low, high, *after, *far, *before)
    weights = [in_hbm(w) for w in weights + tuple(swapped(w) for w in weights)]

    fgain = fast_gain.reshape(1, D)
    own_0, *outs = encode_first(
        flags, mine.reshape(SEQ, 4, LT, 8, 128), enc_gain.reshape(1, D), fgain, weights
    )
    kv_0, carried = tuple(outs[:HEADS]), outs[HEADS:]
    got_0 = tuple(shifted(kv_0[d], d) for d in range(1, HEADS))
    own_1, *kv_1 = encode_second(flags, fgain, *carried, weights)
    kv_1 = tuple(kv_1)
    kv_1, got_0 = lax.optimization_barrier((kv_1, got_0))
    got_1 = tuple(shifted(kv_1[d], d) for d in range(1, HEADS))

    gate_up = fast_gate_up[0]
    down = fast_down[0].T
    sums = fast((kv_0[0], kv_1[0]), (gate_up, down), None, False)
    sums = fast(got_0, (gate_up, down), sums, False)
    qe = query(flags, own_0, own_1, fgain, weights)
    got_1, qe = lax.optimization_barrier((got_1, tuple(qe)))
    grads = fast(got_1, (gate_up, down), sums, True)

    own_qe, up_qe, down_qe = qe
    up_qe, down_qe = shifted(up_qe, 1), shifted(down_qe, -1)
    far_qe = (shifted(up_qe[SPAN:], 1), shifted(down_qe[SPAN:], -1))
    arrived = exchange(grads, SEQ_AXES)
    whole = exchange(sum_pieces(arrived.reshape(SEQ, GT // SEQ, 8, 128)), SEQ_AXES)
    return apply(
        flags,
        whole.reshape(GT, 8, 128),
        gate_up,
        down,
        (own_qe, up_qe, down_qe, *far_qe),
    ).T


def solution(mesh):
    fine = Mesh(mesh.devices.reshape(4, 4, 2, HEADS), ALL_AXES)
    in_specs = (
        P(SEQ_AXES, None),
        P(SEQ_AXES),
        P(SEQ_AXES),
        P(),
        P(None, None, "head"),
        P("head", None),
        P(),
        P(None, None, "head"),
        P(None, "head"),
        P("head", None, None, None),
        P("head", None, None),
    )
    return jax.shard_map(
        on_device, mesh=fine, in_specs=in_specs, out_specs=P(SEQ_AXES, "head"), check_vma=False
    )
```

```python
import jax
import jax.numpy as jnp
from jax import lax
from jax.experimental import pallas as pl
from jax.experimental.pallas import tpu as pltpu
from jax.sharding import Mesh, PartitionSpec as P

D = 768
HDIM = 64
BLK = 256
SPAN = 512
FW = 192
FH = 384
SEQ = 32
HEADS = 4
PAIRS = 8
LT = 3
GT = 224
WROWS = 688
KV_AT = 384
RATE_AT = 576
Q_AT = 592
CUT = 352
EPSILON = 1e-06
LOG2E = 1.4426950408889634
RATE_SCALE = 0.1
VTOKENS = 65536
BF = jnp.bfloat16
F32 = jnp.float32
SEQ_AXES = ("x", "z", "core")
ALL_AXES = ("x", "z", "core", "head")


def params(mib):
    return pltpu.CompilerParams(vmem_limit_bytes=mib << 20)


def cost(us):
    return pl.CostEstimate(flops=0, bytes_accessed=int(us * 3.6e6), transcendentals=0)


ANY = pl.BlockSpec(memory_space=pltpu.HBM)
SMEM = pl.BlockSpec(memory_space=pltpu.SMEM)
VMEM = pl.BlockSpec(memory_space=pltpu.VMEM)


def in_hbm(x):
    return pltpu.with_memory_space_constraint(x, pltpu.HBM)


def mm(a, b):
    return jnp.dot(a, b, preferred_element_type=F32)


def mm_nt(a, b):
    return lax.dot_general(a, b, (((1,), (1,)), ((), ())), preferred_element_type=F32)


def mm_tn(a, b):
    return lax.dot_general(a, b, (((0,), (0,)), ((), ())), preferred_element_type=F32)


def norm(rows, gain):
    factor = lax.rsqrt(jnp.mean(rows * rows, axis=-1, keepdims=True) + EPSILON)
    return (rows * factor * gain).astype(BF)


def spread_body(
    at_ref, dest_hbm, image_hbm, x_ref, rate_hbm, qkv_ref, out_ref, fast_ref,
    o_ref, low_ref, high_ref, buf, o_buf, w_ref, dest_ref, image_ref, rate_ref,
    sems, wsems, osem, psem, ssem,
):
    head = at_ref[1]
    core = at_ref[2]
    parity = lax.shift_right_logical(head, 1)
    half = head & 1
    small = [
        pltpu.make_async_copy(dest_hbm, dest_ref, ssem.at[0]),
        pltpu.make_async_copy(image_hbm, image_ref, ssem.at[1]),
        pltpu.make_async_copy(rate_hbm, rate_ref, ssem.at[2]),
    ]
    for c in small:
        c.start()
    copies = []
    for p in range(PAIRS):
        copies.append(
            pltpu.make_async_copy(
                x_ref.at[
                    pl.ds(p * 64 + parity * 32, SEQ), :, pl.ds(pl.multiple_of(half * FH, 128), FH)
                ],
                buf.at[p],
                sems.at[p],
            )
        )
        copies[p].start()

    def rows(ref, start, count):
        return ref.at[pl.ds(pl.multiple_of(start, 32), count)]

    moves = [
        (rows(qkv_ref, core * 288, 288), w_ref.at[pl.ds(0, 288)]),
        (rows(out_ref, core * 96, 96), w_ref.at[pl.ds(288, 96)]),
        (rows(fast_ref, FW + core * FW, FW), w_ref.at[pl.ds(KV_AT, FW)]),
        (rows(fast_ref, core * 96, 96), w_ref.at[pl.ds(Q_AT, 96)]),
    ]
    moves = [pltpu.make_async_copy(*m, wsems.at[i]) for i, m in enumerate(moves)]
    for m in moves:
        m.start()
    for c in small:
        c.wait()
    w_ref[pl.ds(RATE_AT, 16), :] = jnp.broadcast_to(rate_ref[...], (16, D))
    row = lax.broadcasted_iota(jnp.int32, (8, 128), 0)
    lane = jnp.where(row == 0, lax.broadcasted_iota(jnp.int32, (8, 128), 1), 128)
    tile = jnp.zeros((8, 128), F32)
    for i in range(16):
        tile = jnp.where(lane == i, dest_ref[i].astype(F32), tile)
        tile = jnp.where(lane == 16 + i, image_ref[i].astype(F32), tile)
    o_buf[PAIRS, :, 0] = jnp.broadcast_to(tile.astype(BF)[None], (SEQ, 8, 128))
    puts = [pltpu.make_async_copy(o_buf.at[PAIRS, :, 0], o_ref.at[:, PAIRS * LT], psem.at[PAIRS])]
    puts[0].start()
    for m in moves:
        m.wait()
    outs = [
        pltpu.make_async_copy(w_ref.at[pl.ds(0, CUT)], low_ref, osem.at[0]),
        pltpu.make_async_copy(w_ref.at[pl.ds(CUT, WROWS - CUT)], high_ref, osem.at[1]),
    ]
    for c in outs:
        c.start()
    for p in range(PAIRS):
        copies[p].wait()
        for t in range(LT):
            o_buf[p, :, t] = buf[p, :, :, t * 128 : (t + 1) * 128]
        puts.append(
            pltpu.make_async_copy(o_buf.at[p], o_ref.at[:, pl.ds(p * LT, LT)], psem.at[p])
        )
        puts[-1].start()
    for c in outs + puts:
        c.wait()


def spread(at, dest, image, x, rate, *weights):
    return pl.pallas_call(
        spread_body,
        out_shape=(
            pltpu.HBM((SEQ, PAIRS * LT + 1, 8, 128), BF),
            pltpu.HBM((CUT, D), BF),
            pltpu.HBM((WROWS - CUT, D), BF),
        ),
        in_specs=[SMEM] + [ANY] * 7,
        out_specs=[ANY] * 3,
        scratch_shapes=[
            pltpu.VMEM((PAIRS, SEQ, 8, FH), BF),
            pltpu.VMEM((PAIRS + 1, SEQ, LT, 8, 128), BF),
            pltpu.VMEM((WROWS, D), BF),
            pltpu.SMEM((16,), jnp.int32),
            pltpu.SMEM((16,), jnp.int32),
            pltpu.VMEM((1, D), BF),
            pltpu.SemaphoreType.DMA((PAIRS,)),
            pltpu.SemaphoreType.DMA((4,)),
            pltpu.SemaphoreType.DMA((2,)),
            pltpu.SemaphoreType.DMA((PAIRS + 1,)),
            pltpu.SemaphoreType.DMA((3,)),
        ],
        compiler_params=params(12),
        cost_estimate=cost(3),
        name="spread",
    )(at, *[in_hbm(a) for a in (dest, image, x, rate, *weights)])


def pick_body(at_ref, x_ref, o_ref, flag_ref, ids, table, source, sem):
    ids[...] = x_ref[:, PAIRS * LT, 0, :].astype(F32).astype(jnp.int32)
    copy = pltpu.make_async_copy(ids, table, sem)
    copy.start()
    copy.wait()

    def note(i, carry):
        for p in range(PAIRS):
            first = table[i, 2 * p]
            pair = jnp.minimum(lax.shift_right_arithmetic(first, 1), SEQ * HEADS - 1)
            source[jnp.where(first >= 0, pair, SEQ * HEADS)] = i * PAIRS + p
        return carry

    lax.fori_loop(0, SEQ, note, 0, unroll=2)

    def move(m, carry):
        q = source[m]
        at = (q & (PAIRS - 1)) * LT
        o_ref[m] = x_ref[lax.shift_right_logical(q, 3), pl.ds(at, LT)]
        return carry

    lax.fori_loop(0, SEQ * HEADS, move, 0, unroll=16)
    q = source[at_ref[0]]
    origin = lax.shift_right_logical(q, 3)
    slot = (q & (PAIRS - 1)) * 2
    flag_ref[0] = table[origin, slot] & 1
    flag_ref[1] = jnp.where(table[origin, 16 + slot] == table[origin, 17 + slot], 1, 0)
    flag_ref[2] = at_ref[1]
    flag_ref[3] = at_ref[2]


def pick(at, x):
    return pl.pallas_call(
        pick_body,
        out_shape=(
            jax.ShapeDtypeStruct((SEQ * HEADS, LT, 8, 128), BF),
            jax.ShapeDtypeStruct((4,), jnp.int32),
        ),
        in_specs=[SMEM, VMEM],
        out_specs=[VMEM, SMEM],
        scratch_shapes=[
            pltpu.VMEM((SEQ, 128), jnp.int32),
            pltpu.SMEM((SEQ, 128), jnp.int32),
            pltpu.SMEM((SEQ * HEADS + 8,), jnp.int32),
            pltpu.SemaphoreType.DMA(()),
        ],
        compiler_params=params(8),
        cost_estimate=cost(3),
        name="pick",
    )(at, x)


def weight_copies(core, w_refs, d, start, count, dst, sem):
    copies = []
    low = max(0, min(count, CUT - start))
    for side in range(2):
        to = dst.at[core if side == 0 else 1 - core]
        low_ref, high_ref = w_refs[side * 8 + d * 2 : side * 8 + d * 2 + 2]
        pieces = [(low_ref, start, 0, low), (high_ref, start + low - CUT, low, count - low)]
        for ref, at, put, n in pieces:
            if n:
                copies.append(
                    pltpu.make_async_copy(ref.at[pl.ds(at, n)], to.at[pl.ds(put, n)], sem)
                )
    return copies


def wait_all(dst, sem):
    pltpu.make_async_copy(dst, dst, sem).wait()


def attend(block, bias, q, k, v):
    lane = lax.broadcasted_iota(jnp.int32, (BLK, FW), 1)
    out = None
    for j in range(FW // HDIM):
        mine = (lane >= j * HDIM) & (lane < (j + 1) * HDIM)
        s = mm_nt(jnp.where(mine, q, jnp.zeros_like(q)), k)
        parts = [s[:, :BLK], s[:, BLK:]]
        parts[1 - block] = parts[1 - block] + bias
        top = jnp.max(jnp.maximum(parts[0], parts[1]), axis=-1, keepdims=True)
        p = jnp.concatenate([jnp.exp2(x - top).astype(BF) for x in parts], axis=1)
        o = mm(p, v)
        o = o[:, :FW] * (1.0 / o[:, FW : FW + 1])
        out = o if out is None else jnp.where(mine, o, out)
    return out.astype(BF)


def project(block, gain, fs, fsems, kv_refs):
    n = norm(block.astype(F32), gain)
    lane = lax.broadcasted_iota(jnp.int32, (BLK, 2 * FW), 1)
    for d in range(HEADS):
        wait_all(fs.at[d], fsems.at[d])
    z = mm_nt(n, jnp.concatenate([fs[d, 0, FW:] for d in range(HEADS)], axis=0))
    soft = jnp.maximum(z, 0.0) + jnp.log1p(jnp.exp(-jnp.abs(z)))
    rates = -(RATE_SCALE * VTOKENS**-0.5) * soft
    for d, kv_ref in enumerate(kv_refs):
        kv = mm_nt(n, fs[d, :, :FW].reshape(2 * FW, D)).astype(BF).astype(F32)
        kv_ref[...] = jnp.where(lane < FW, kv, kv * rates[:, d * 16 : d * 16 + 1]).astype(BF)


def encode_first_body(
    flag_ref, x_ref, gain_ref, fgain_ref, *refs
):
    w_refs = refs[:16]
    o_ref, kv0, kv1, kv2, kv3, q_ref, k_ref, v_ref, rest_ref = refs[16:25]
    xs, ns, ws, fs, sems, fsems = refs[25:]
    core = flag_ref[3]
    for d in range(HEADS):
        for c in weight_copies(core, w_refs, d, 0, FH, ws.at[d], sems.at[d]):
            c.start()
    for d in range(HEADS):
        for c in weight_copies(core, w_refs, d, KV_AT, FW + 16, fs.at[d], fsems.at[d]):
            c.start()
    flip = flag_ref[0]
    bias = jnp.where(flag_ref[1] != 0, 0.0, -1e30).astype(F32)
    for b in range(2):
        base = pl.multiple_of(jnp.bitwise_xor(flip, b) * BLK, BLK)
        for c in range(2):
            for t in range(LT):
                xs[pl.ds(base, BLK), pl.ds(c * FH + t * 128, 128)] = (
                    x_ref[:, 2 * b + c, t].astype(F32).reshape(BLK, 128)
                )
    gain = gain_ref[...]
    for r in range(8):
        ns[pl.ds(r * 64, 64), :] = norm(xs[pl.ds(r * 64, 64), :], gain)
    rest_ref[...] = xs[BLK:, :].astype(BF)
    n = ns[...]
    scale = HDIM**-0.5 * LOG2E
    out = xs[:BLK, :]
    for g in range(HEADS):
        wait_all(ws.at[g], sems.at[g])
        w = ws[g, :, : 3 * 96].reshape(3 * FW, D)
        q = (mm_nt(n, w[:FW]) * scale).astype(BF)
        k = mm_nt(n, w[FW : 2 * FW]).astype(BF)
        v = jnp.concatenate(
            [mm_nt(n, w[2 * FW :]).astype(BF), jnp.ones((SPAN, HDIM), BF)], axis=1
        )
        q_ref[g] = q[BLK:]
        k_ref[g] = k
        v_ref[g] = v
        att = attend(0, bias, q[:BLK], k, v)
        out = out + mm(att, ws[g, :, 3 * 96 :].reshape(FW, D))
    out = out.astype(BF)
    o_ref[...] = out
    project(out, fgain_ref[...], fs, fsems, (kv0, kv1, kv2, kv3))


def encode_first(flags, x, gain, fgain, weights):
    return pl.pallas_call(
        encode_first_body,
        out_shape=(
            jax.ShapeDtypeStruct((BLK, D), BF),
            *[jax.ShapeDtypeStruct((BLK, 2 * FW), BF)] * HEADS,
            jax.ShapeDtypeStruct((HEADS, BLK, FW), BF),
            jax.ShapeDtypeStruct((HEADS, SPAN, FW), BF),
            jax.ShapeDtypeStruct((HEADS, SPAN, FW + HDIM), BF),
            jax.ShapeDtypeStruct((BLK, D), BF),
        ),
        in_specs=[SMEM, VMEM, VMEM, VMEM] + [ANY] * 16,
        out_specs=[VMEM] * 9,
        scratch_shapes=[
            pltpu.VMEM((SPAN, D), F32),
            pltpu.VMEM((SPAN, D), BF),
            pltpu.VMEM((HEADS, 2, FH, D), BF),
            pltpu.VMEM((HEADS, 2, FW + 16, D), BF),
            pltpu.SemaphoreType.DMA((HEADS,)),
            pltpu.SemaphoreType.DMA((HEADS,)),
        ],
        compiler_params=params(24),
        cost_estimate=cost(9),
        name="encode_first",
    )(flags, x, gain, fgain, *weights)


def encode_second_body(
    flag_ref, fgain_ref, q_ref, k_ref, v_ref, rest_ref, *refs
):
    w_refs = refs[:16]
    o_ref, kv0, kv1, kv2, kv3, ws, fs, sem, fsems = refs[16:]
    core = flag_ref[3]
    for d in range(HEADS):
        for c in weight_copies(core, w_refs, d, 3 * 96, 96, ws.at[d], sem):
            c.start()
    for d in range(HEADS):
        for c in weight_copies(core, w_refs, d, KV_AT, FW + 16, fs.at[d], fsems.at[d]):
            c.start()
    bias = jnp.where(flag_ref[1] != 0, 0.0, -1e30).astype(F32)
    out = rest_ref[...].astype(F32)
    for g in range(HEADS):
        att = attend(1, bias, q_ref[g], k_ref[g], v_ref[g])
        if g == 0:
            wait_all(ws, sem)
        out = out + mm(att, ws[g].reshape(FW, D))
    out = out.astype(BF)
    o_ref[...] = out
    project(out, fgain_ref[...], fs, fsems, (kv0, kv1, kv2, kv3))


def encode_second(flags, fgain, q, k, v, rest, weights):
    return pl.pallas_call(
        encode_second_body,
        out_shape=(
            jax.ShapeDtypeStruct((BLK, D), BF),
            *[jax.ShapeDtypeStruct((BLK, 2 * FW), BF)] * HEADS,
        ),
        in_specs=[SMEM] + [VMEM] * 5 + [ANY] * 16,
        out_specs=[VMEM] * 5,
        scratch_shapes=[
            pltpu.VMEM((HEADS, 2, 96, D), BF),
            pltpu.VMEM((HEADS, 2, FW + 16, D), BF),
            pltpu.SemaphoreType.DMA(()),
            pltpu.SemaphoreType.DMA((HEADS,)),
        ],
        compiler_params=params(16),
        cost_estimate=cost(20),
        name="encode_second",
    )(flags, fgain, q, k, v, rest, *weights)


def query_body(flag_ref, x0_ref, x1_ref, gain_ref, *refs):
    w_refs = refs[:16]
    own_ref, up_ref, down_ref, ws, sems = refs[16:]
    whole = {0: own_ref, 1: up_ref, 3: down_ref}
    head = flag_ref[2]
    for d in range(HEADS):
        for c in weight_copies(flag_ref[3], w_refs, d, Q_AT, 96, ws.at[d], sems.at[d]):
            c.start()
    xs = (x0_ref[...], x1_ref[...])
    ns = [norm(x.astype(F32), gain_ref[...]) for x in xs]
    cols = [[x[:, g * FW : (g + 1) * FW] for g in range(HEADS)] for x in xs]
    for d in range(HEADS):
        there = ((head + d) & (HEADS - 1))
        wait_all(ws.at[d], sems.at[d])
        w = ws[d].reshape(FW, D)
        for i in range(2):
            q = mm_nt(ns[i], w).astype(BF)
            c = cols[i]
            e = jnp.where(
                there < 2, jnp.where(there == 0, c[0], c[1]), jnp.where(there == 2, c[2], c[3])
            )
            qe = jnp.concatenate([q, e], axis=1)
            if d == 2:
                (up_ref, down_ref)[i][SPAN:, :] = qe
            else:
                whole[d][pl.ds(i * BLK, BLK), :] = qe


def query(flags, x0, x1, gain, weights):
    return pl.pallas_call(
        query_body,
        out_shape=(
            jax.ShapeDtypeStruct((SPAN, 2 * FW), BF),
            jax.ShapeDtypeStruct((SPAN + BLK, 2 * FW), BF),
            jax.ShapeDtypeStruct((SPAN + BLK, 2 * FW), BF),
        ),
        in_specs=[SMEM, VMEM, VMEM, VMEM] + [ANY] * 16,
        out_specs=[VMEM] * 3,
        scratch_shapes=[
            pltpu.VMEM((HEADS, 2, 96, D), BF),
            pltpu.SemaphoreType.DMA((HEADS,)),
        ],
        compiler_params=params(12),
        cost_estimate=cost(4),
        name="fast_query",
    )(flags, x0, x1, gain, *weights)


def make_fast_body(blocks, first, last):
    def body(*refs):
        kv_refs = refs[:blocks]
        gu_ref, down_ref = refs[blocks : blocks + 2]
        sum_ref = None if first else refs[blocks + 2]
        g_ref = refs[-1]
        gate_up = [gu_ref[i].astype(BF) for i in range(2)]
        down = down_ref[...].astype(BF)
        sums = None
        for kv_ref in kv_refs:
            key = kv_ref[:, :FW]
            out_grad = kv_ref[:, FW:]
            gate = mm(key, gate_up[0])
            up = mm(key, gate_up[1])
            hidden_grad = mm(out_grad, down)
            s = jax.nn.sigmoid(gate)
            silu = gate * s
            hidden = (silu * up).astype(BF)
            gate_grad = (hidden_grad * up * s * (1.0 + gate * (1.0 - s))).astype(BF)
            up_grad = (hidden_grad * silu).astype(BF)
            parts = [mm_tn(key, gate_grad), mm_tn(key, up_grad), mm_tn(out_grad, hidden)]
            sums = parts if sums is None else [a + b for a, b in zip(sums, parts)]
        for i, total in enumerate(sums):
            if not first:
                total = total + sum_ref[i]
            if last:
                for t in range(LT):
                    g_ref[pl.ds((i * LT + t) * 24, 24)] = (
                        total[:, t * 128 : (t + 1) * 128].astype(BF).reshape(24, 8, 128)
                    )
            else:
                g_ref[i] = total
        if last:
            g_ref[pl.ds(216, 8)] = jnp.zeros((8, 8, 128), BF)

    return body


def fast(blocks, shared, sums, last):
    first = sums is None
    operands = (*blocks, *shared) + (() if first else (sums,))
    return pl.pallas_call(
        make_fast_body(len(blocks), first, last),
        out_shape=(
            jax.ShapeDtypeStruct((GT, 8, 128), BF)
            if last
            else jax.ShapeDtypeStruct((3, FW, FH), F32)
        ),
        in_specs=[VMEM] * len(operands),
        out_specs=VMEM,
        compiler_params=params(16),
        cost_estimate=cost(3),
        name="fast_grad",
    )(*operands)


def sum_body(x_ref, o_ref):
    total = x_ref[0].astype(F32)
    for i in range(1, SEQ):
        total = total + x_ref[i].astype(F32)
    total = total.astype(BF)
    for i in range(SEQ):
        o_ref[i] = total


def sum_pieces(x):
    return pl.pallas_call(
        sum_body,
        out_shape=jax.ShapeDtypeStruct(x.shape, BF),
        in_specs=[VMEM],
        out_specs=VMEM,
        compiler_params=params(4),
        cost_estimate=cost(1),
        name="sum_pieces",
    )(x)


def renorm(updated, initial, axis):
    target = jnp.sqrt(jnp.sum(initial * initial, axis=axis, keepdims=True))
    return updated * target * lax.rsqrt(jnp.sum(updated * updated, axis=axis, keepdims=True) + EPSILON)


def apply_body(head_ref, g_ref, gu_ref, down_ref, *refs):
    qe_refs, (o_ref, o_buf, gs, ws, sems) = refs[:5], refs[5:]
    for i in range(3):
        for t in range(LT):
            gs[i, :, pl.ds(t * 128, 128)] = (
                g_ref[pl.ds((i * LT + t) * 24, 24)].astype(F32).reshape(FW, 128)
            )
        init = down_ref[...] if i == 2 else gu_ref[i]
        ws[i] = renorm(init - gs[i], init, 0 if i == 2 else 1).astype(BF)
    row = lax.broadcasted_iota(jnp.int32, (FW, 2 * FW - 128), 0)
    col = lax.broadcasted_iota(jnp.int32, (FW, 2 * FW - 128), 1)
    columns = jnp.where(row + FW - 128 == col, 1.0, 0.0).astype(BF)
    own_ref, up_ref, down_side_ref, far0_ref, far1_ref = qe_refs
    puts = []
    for d in (0, 1, 3, 2):
        if d == 2:
            qe = jnp.concatenate([far0_ref[...], far1_ref[...]], axis=0)
        else:
            qe = {0: own_ref, 1: up_ref, 3: down_side_ref}[d][:SPAN, :]
        q = qe[:, :FW]
        gate = mm(q, ws[0])
        hidden = (gate * jax.nn.sigmoid(gate) * mm(q, ws[1])).astype(BF)
        base = pl.multiple_of(((head_ref[2] + HEADS - d) & (HEADS - 1)) * SPAN, SPAN)
        o_buf[d] = (mm_nt(columns, qe[:, 128:]) + mm_nt(ws[2], hidden)).astype(BF)
        puts.append(
            pltpu.make_async_copy(o_buf.at[d], o_ref.at[:, pl.ds(base, SPAN)], sems.at[d])
        )
        puts[-1].start()
    for c in puts:
        c.wait()


def apply(flags, grads, gate_up, down, qes):
    return pl.pallas_call(
        apply_body,
        out_shape=pltpu.HBM((FW, HEADS * SPAN), BF),
        in_specs=[SMEM] + [VMEM] * 8,
        out_specs=ANY,
        scratch_shapes=[
            pltpu.VMEM((HEADS, FW, SPAN), BF),
            pltpu.VMEM((3, FW, FH), F32),
            pltpu.VMEM((3, FW, FH), BF),
            pltpu.SemaphoreType.DMA((HEADS,)),
        ],
        compiler_params=params(16),
        cost_estimate=cost(3),
        name="apply_fast",
    )(flags, grads, gate_up, down, *qes)


def exchange(x, axes):
    return lax.all_to_all(x, axes, split_axis=0, concat_axis=0, tiled=True)


def shifted(x, by):
    return lax.ppermute(x, "head", [(i, (i + by) % HEADS) for i in range(HEADS)])


def swapped(x):
    return lax.ppermute(x, "core", [(0, 1), (1, 0)])


def on_device(
    patches,
    slot_image,
    slot_dest,
    enc_gain,
    w_qkv,
    w_out,
    fast_gain,
    w_fast,
    w_rate,
    fast_gate_up,
    fast_down,
):
    head = lax.axis_index("head")
    core = lax.axis_index("core")
    seq = lax.axis_index(SEQ_AXES)
    at = jnp.stack([seq * HEADS + head, head, core]).astype(jnp.int32)

    pieces, low, high = spread(
        at,
        slot_dest,
        slot_image,
        patches.reshape(-1, 8, D),
        w_rate.T,
        jnp.transpose(w_qkv, (0, 2, 1)).reshape(3 * FW, D),
        w_out,
        jnp.transpose(w_fast, (0, 2, 1)).reshape(3 * FW, D),
    )
    after_high, before_low = shifted(high, -1), shifted(low, 1)
    after = (shifted(low, -1), after_high)
    before = (before_low, shifted(high, 1))
    picked, flags = pick(at, exchange(pieces, SEQ_AXES))
    mine = exchange(picked, ALL_AXES)
    far = (shifted(before[0], 1), shifted(after[1], -1))
    weights = (low, high, *after, *far, *before)
    weights = [in_hbm(w) for w in weights + tuple(swapped(w) for w in weights)]

    fgain = fast_gain.reshape(1, D)
    own_0, *outs = encode_first(
        flags, mine.reshape(SEQ, 4, LT, 8, 128), enc_gain.reshape(1, D), fgain, weights
    )
    kv_0, carried = tuple(outs[:HEADS]), outs[HEADS:]
    got_0 = tuple(shifted(kv_0[d], d) for d in range(1, HEADS))
    own_1, *kv_1 = encode_second(flags, fgain, *carried, weights)
    kv_1 = tuple(kv_1)
    kv_1, got_0 = lax.optimization_barrier((kv_1, got_0))
    got_1 = tuple(shifted(kv_1[d], d) for d in range(1, HEADS))

    gate_up = fast_gate_up[0]
    down = fast_down[0].T
    sums = fast((kv_0[0], kv_1[0]), (gate_up, down), None, False)
    sums = fast(got_0, (gate_up, down), sums, False)
    qe = query(flags, own_0, own_1, fgain, weights)
    got_1, qe = lax.optimization_barrier((got_1, tuple(qe)))
    grads = fast(got_1, (gate_up, down), sums, True)

    own_qe, up_qe, down_qe = qe
    up_qe, down_qe = shifted(up_qe, 1), shifted(down_qe, -1)
    far_qe = (shifted(up_qe[SPAN:], 1), shifted(down_qe[SPAN:], -1))
    arrived = exchange(grads, SEQ_AXES)
    whole = exchange(sum_pieces(arrived.reshape(SEQ, GT // SEQ, 8, 128)), SEQ_AXES)
    return apply(
        flags,
        whole.reshape(GT, 8, 128),
        gate_up,
        down,
        (own_qe, up_qe, down_qe, *far_qe),
    ).T


def solution(mesh):
    fine = Mesh(mesh.devices.reshape(4, 4, 2, HEADS), ALL_AXES)
    in_specs = (
        P(SEQ_AXES, None),
        P(SEQ_AXES),
        P(SEQ_AXES),
        P(),
        P(None, None, "head"),
        P("head", None),
        P(),
        P(None, None, "head"),
        P(None, "head"),
        P("head", None, None, None),
        P("head", None, None),
    )
    return jax.shard_map(
        on_device, mesh=fine, in_specs=in_specs, out_specs=P(SEQ_AXES, "head"), check_vma=False
    )
```
